32 devices in a mesh: depth: 2 (over y), tile: 16 (over z, x, core).
Axes of the slice: x: 2, y: 2, z: 4, core: 2. Of those that a mesh axis runs over, the one named last changes fastest.
Arguments:
- density: float32 [2, 128, 4096], P('depth', None, 'tile'), may hold values from 0.5 to 2
- prior: float32 [2, 128, 4096], P('depth', None, 'tile'), may hold values from 0.5 to 2
- observed: float32 [6, 128, 4096], P(None, None, 'tile'), may hold values from -6 to 6
- filter_across: float32 [2, 6, 4, 33], P('depth'), may hold values from -1 to 1
- filter_along: float32 [2, 6, 4, 33], P('depth'), may hold values from -0.375 to 0.375
- comp_weight: float32 [6], replicated, may hold values from 0.5 to 2
Outputs:
- gradient: float32 [2, 128, 4096], P('depth', None, 'tile')
- residual: float32 [6, 128, 4096], P(None, 'depth', 'tile')
The draws below stay inside these ranges and needn't reach their ends.
All inputs are finite; a program needn't handle non-finite values.
Results may differ from the reference program's by a relative error of at most 0.0001.
Values sent between devices are 32-bit elements; how exact they have to be, the bound alone decides.
No kernel may reach another device: no remote copies, remote signals or barrier semaphores. Data moves between devices by JAX's collectives and lax.ppermute only.
A program may use at most 128 MiB of HBM per device.

```python
import math
import jax
import jax.numpy as jnp
from jax import lax

NX = 128
COMPS = 6
RANK = 4
TAPS = 33
LAYERS = 2
NY = 4096


def block_levels(stream_key, shape, cuts, smallest, top_value):
    def one(axis_at, parts):
        steps = jax.random.uniform(jax.random.fold_in(jax.random.fold_in(stream_key, 6), axis_at), (parts,), jnp.float32, smallest / len(cuts), top_value / len(cuts))
        return jnp.repeat(jnp.exp(steps), shape[axis_at] // parts).reshape((-1,) + (1,) * (len(shape) - axis_at - 1))

    level = one(*cuts[0])
    for cut in cuts[1:]:
        level = level * one(*cut)
    return level


def gaussian(own_key, dims, spread, most, pieces=(), dtype=jnp.bfloat16):
    values = jax.random.normal(own_key, dims, jnp.float32) * spread
    if len(pieces) > 0:
        values = block_levels(own_key, dims, pieces, -0.22, 0.18) * values
    return jnp.clip(values, min=-most, max=most).astype(dtype)


def setup_inputs(seed: int = 0) -> dict:
    splits = jax.random.split(jax.random.key(seed), 7)
    return {
        "density": jnp.clip(jnp.exp(math.log(2.0) - 1.3862944 * jax.random.uniform(splits[0], (LAYERS, NX, NY), jnp.float32) ** block_levels(splits[0], (LAYERS, NX, NY), ((0, 2), (2, 16)), -0.2, 0.2)), 0.5, 2.0),
        "prior": jnp.clip(jnp.exp(math.log(2.0) - 1.3862944 * jax.random.uniform(splits[1], (LAYERS, NX, NY), jnp.float32) ** block_levels(splits[1], (LAYERS, NX, NY), ((0, 2), (2, 16)), -0.2, 0.2)), 0.5, 2.0),
        "observed": gaussian(splits[2], (COMPS, NX, NY), 1.0, 6.0, ((2, 16),), jnp.float32),
        "filter_across": gaussian(splits[3], (LAYERS, COMPS, RANK, TAPS), TAPS ** -0.5, 1.0, ((0, 2),), jnp.float32),
        "filter_along": gaussian(splits[4], (LAYERS, COMPS, RANK, TAPS), (TAPS * RANK * LAYERS) ** -0.5, 0.375, ((0, 2),), jnp.float32),
        "comp_weight": jnp.clip(jnp.exp(jax.random.uniform(splits[5], (COMPS,), jnp.float32, math.log(0.5), math.log(2.0))), 0.5, 2.0),
    }


PRECISE = lax.Precision.HIGHEST
PRIOR_WEIGHT = 0.5


def band_rows(filters, extent):
    center = filters.shape[-1] // 2
    offsets = jnp.arange(extent)[None, :] - jnp.arange(extent)[:, None] + center
    indicator = (offsets[:, :, None] == jnp.arange(filters.shape[-1])[None, None, :]).astype(jnp.float32)
    return jnp.einsum("ijk,bk->bij", indicator, filters, precision=PRECISE)


def shifted(field, extent):
    return jnp.stack([lax.slice_in_dim(field, offset, offset + extent, axis=field.ndim - 1) for offset in range(TAPS)])


def reference(density, prior, observed, filter_across, filter_along, comp_weight):
    margin = TAPS // 2
    padded = jnp.pad(density, ((0, 0), (0, 0), (margin, margin)))

    def forward_layer(summed, inputs):
        layer_field, across, along = inputs
        stacks = shifted(layer_field, NY)
        smooth = jnp.einsum("kxq,crk->crxq", stacks, along, precision=PRECISE)
        banded = band_rows(across.reshape(COMPS * RANK, TAPS), NX).reshape(COMPS, RANK, NX, NX)
        return summed + jnp.einsum("crij,crjq->ciq", banded, smooth, precision=PRECISE), None

    response, unused = lax.scan(forward_layer, jnp.zeros((COMPS, NX, NY), jnp.float32), (padded, filter_across, filter_along))
    residual = (response - observed) * comp_weight[:, None, None]
    padded_res = jnp.pad(residual, ((0, 0), (0, 0), (margin, margin)))

    def adjoint_layer(inputs):
        across, along = inputs
        banded = band_rows(across.reshape(COMPS * RANK, TAPS), NX).reshape(COMPS, RANK, NX, NX)
        summed = jnp.zeros((NX, NY), jnp.float32)
        for component in range(COMPS):
            stacks = shifted(padded_res[component], NY)
            smooth = jnp.einsum("kxq,rk->rxq", stacks, along[component, :, ::-1], precision=PRECISE)
            summed = summed + jnp.einsum("rij,riq->jq", banded[component], smooth, precision=PRECISE)
        return summed

    adjoint = lax.map(adjoint_layer, (filter_across, filter_along))
    gradient = adjoint + PRIOR_WEIGHT * (jnp.log(density) - jnp.log(prior))
    return gradient, residual
```

```python
import jax
import jax.numpy as jnp
from jax import lax
from jax.experimental import pallas as pl
from jax.experimental.pallas import tpu as pltpu
from jax.sharding import PartitionSpec as P

COMPS = 6
RANK = 4
TAPS = 33
MARGIN = 16
HALO = 32
BLOCK = 32
FILTERS = COMPS * RANK
PRIOR_WEIGHT = 0.5
F32 = jnp.float32
BF16 = jnp.bfloat16


def split(x):
    hi = x.astype(BF16)
    return hi, (x - hi.astype(F32)).astype(BF16)


def parity():
    return lax.rem(lax.axis_index("tile"), 2) == 0


def pack_kernel(d_ref, o_ref, fa_ref, fl_ref, e_ref, out_ref, ed_ref, od_ref):
    width = d_ref.shape[2]
    even = parity()
    first = d_ref[0, :, 0:128].T[0:HALO]
    last = d_ref[0, :, width - 128 : width].T[128 - HALO : 128]
    to_e = jnp.where(even, last, first)
    to_o = jnp.where(even, first, last)
    e_ref[0:HALO, :] = to_e
    out_ref[0:HALO, :] = to_o
    ed_ref[0:HALO, :] = to_e
    od_ref[...] = to_o
    for c in range(COMPS):
        first = o_ref[c, :, 0:128].T[0:MARGIN]
        last = o_ref[c, :, width - 128 : width].T[128 - MARGIN : 128]
        rows = slice(HALO + MARGIN * c, HALO + MARGIN * (c + 1))
        e_ref[rows, :] = jnp.where(even, last, first)
        out_ref[rows, :] = jnp.where(even, first, last)
    ed_ref[HALO : HALO + 2 * FILTERS, :] = jnp.zeros((2 * FILTERS, 128), F32)
    for c in range(COMPS):
        rows = slice(HALO + RANK * c, HALO + RANK * (c + 1))
        ed_ref[rows, 0:TAPS] = fa_ref[0, c]
        rows = slice(HALO + FILTERS + RANK * c, HALO + FILTERS + RANK * (c + 1))
        ed_ref[rows, 0:TAPS] = fl_ref[0, c]


def pack(density, observed, across, along):
    msg = HALO + COMPS * MARGIN
    return pl.pallas_call(
        pack_kernel,
        out_shape=[
            jax.ShapeDtypeStruct((msg, 128), F32),
            jax.ShapeDtypeStruct((msg, 128), F32),
            jax.ShapeDtypeStruct((HALO + 2 * FILTERS, 128), F32),
            jax.ShapeDtypeStruct((HALO, 128), F32),
        ],
        name="pack",
    )(density, observed, across, along)


def place(filters, targets):
    tap = lax.broadcasted_iota(jnp.int32, (128, 128), 0)
    lane = lax.broadcasted_iota(jnp.int32, (128, 128), 1)
    chosen = jnp.zeros((128, 128), jnp.bool_)
    for target in targets(tap):
        chosen = chosen | (lane == target)
    chosen = (chosen & (tap < TAPS)).astype(BF16)
    hi, lo = split(filters)
    put = lambda v: jnp.dot(v, chosen, preferred_element_type=F32)
    return put(hi), put(lo)


def main_kernel(layers, *refs):
    it = iter(refs)
    take = lambda k: [next(it) for _ in range(k)]
    dens = take(layers)
    (prior_ref, obs_ref, fa_ref, fl_ref, w_ref, e_ref, o_ref) = take(7)
    eds = take(layers - 1)
    ods = take(layers - 1)
    grad_ref, res_ref = take(2)
    (dhi, dlo, tf, zf, tb, zb, shi, slo, rhi, rlo, bhi, blo, filt, base, turned) = take(15)
    tile = lax.axis_index("tile")
    tiles = lax.axis_size("tile")
    even = lax.rem(tile, 2) == 0
    width = dens[0].shape[2]
    padded = width + 2 * MARGIN
    blocks = padded // BLOCK
    has_left = tile > 0
    has_right = tile < tiles - 1

    filt[...] = jnp.zeros(filt.shape, F32)
    for c in range(COMPS):
        filt[0, 0, RANK * c : RANK * (c + 1), 0:TAPS] = fa_ref[0, c]
        filt[0, 1, RANK * c : RANK * (c + 1), 0:TAPS] = fl_ref[0, c]
    for l in range(1, layers):
        filt[l, 0] = eds[l - 1][HALO : HALO + FILTERS, :]
        filt[l, 1] = eds[l - 1][HALO + FILTERS : HALO + 2 * FILTERS, :]

    for l in range(layers):
        from_e = e_ref[0:HALO, :] if l == 0 else eds[l - 1][0:HALO, :]
        from_o = o_ref[0:HALO, :] if l == 0 else ods[l - 1][...]
        left = jnp.where(has_left, jnp.where(even, from_o, from_e), 0.0)
        right = jnp.where(has_right, jnp.where(even, from_e, from_o), 0.0)
        hi, lo = split(left)
        dhi[l, 0:HALO, :] = hi
        dlo[l, 0:HALO, :] = lo
        hi, lo = split(right)
        dhi[l, HALO + width : 2 * HALO + width, :] = hi
        dlo[l, HALO + width : 2 * HALO + width, :] = lo
        hi, lo = split(dens[l][0].T)
        dhi[l, HALO : HALO + width, :] = hi
        dlo[l, HALO : HALO + width, :] = lo

    row = lax.broadcasted_iota(jnp.int32, (128, 128), 0)
    lane = lax.broadcasted_iota(jnp.int32, (128, 128), 1)
    band = jnp.abs(row - lane) <= MARGIN

    def along_blocks(dst, hi, lo):
        base[0, 0:FILTERS, :] = hi
        base[1, 0:FILTERS, :] = lo
        for f in range(FILTERS):
            for p in range(2):
                v = jnp.broadcast_to(base[p, f : f + 1, :], (BLOCK, 128))
                v = pltpu.roll(v, 0, 1, stride=1, stride_axis=0)
                dst[BLOCK * f : BLOCK * (f + 1), 128 * p : 128 * (p + 1)] = v.astype(BF16)

    def across_blocks(store, hi, lo):
        base[0, 0:FILTERS, :] = hi
        base[1, 0:FILTERS, :] = lo
        for f in range(FILTERS):
            for p in range(2):
                v = jnp.broadcast_to(base[p, f : f + 1, :], (128, 128))
                v = pltpu.roll(v, 0, 1, stride=1, stride_axis=0)
                store(f, p, jnp.where(band, v, 0.0).astype(BF16))

    for l in range(layers):
        along_blocks(tf.at[l], *place(filt[l, 1], lambda k: (k, k + 64)))

        def store_f(f, p, v, l=l):
            c, r = divmod(f, RANK)
            at = 128 * (RANK * l + r)
            zf[c, at : at + 128, 128 * p : 128 * (p + 1)] = v

        across_blocks(store_f, *place(filt[l, 0], lambda k: ((MARGIN - k) & 127,)))

    along_blocks(tb, *place(filt[0, 1], lambda k: (TAPS - 1 - k, TAPS - 1 - k + 64)))

    def store_b(f, p, v):
        zb[128 * f : 128 * (f + 1), 128 * p : 128 * (p + 1)] = v

    across_blocks(store_b, *place(filt[0, 0], lambda k: ((k - MARGIN) & 127,)))

    def stacked(hi, lo, block_list):
        cols = []
        for b in block_list:
            h = hi[BLOCK * b : BLOCK * b + 64, :]
            w = lo[BLOCK * b : BLOCK * b + 64, :]
            cols.append(jnp.concatenate([h, w, h, w], axis=0))
        return jnp.concatenate(cols, axis=1) if len(cols) > 1 else cols[0]

    for l in range(layers):
        for b in range(0, blocks, 2):
            group = [b, b + 1] if b + 1 < blocks else [b]
            rhs = stacked(dhi.at[l], dlo.at[l], group)
            out = jnp.dot(tf[l], rhs, preferred_element_type=F32)
            hi, lo = split(out)
            for i, bb in enumerate(group):
                for f in range(FILTERS):
                    c, r = divmod(f, RANK)
                    at = 128 * (RANK * l + r)
                    rows = slice(BLOCK * bb, BLOCK * (bb + 1))
                    shi[c, rows, at : at + 128] = hi[BLOCK * f : BLOCK * (f + 1), 128 * i : 128 * (i + 1)]
                    slo[c, rows, at : at + 128] = lo[BLOCK * f : BLOCK * (f + 1), 128 * i : 128 * (i + 1)]

    first_row = lax.axis_index("depth") * res_ref.shape[1]
    for c in range(COMPS):
        out = jnp.dot(shi[c], zf[c], preferred_element_type=F32)
        out = out + jnp.dot(slo[c], zf[c], preferred_element_type=F32)
        response = out[:, 0:128] + out[:, 128:256]
        w = w_ref[c]
        center = (response[MARGIN : MARGIN + width] - obs_ref[c].T) * w
        rows = slice(HALO + MARGIN * c, HALO + MARGIN * (c + 1))
        from_e = e_ref[rows, :]
        from_o = o_ref[rows, :]
        left = jnp.where(even, from_o, from_e)
        right = jnp.where(even, from_e, from_o)
        left = jnp.where(has_left, (response[0:MARGIN] - left) * w, 0.0)
        right = jnp.where(has_right, (response[MARGIN + width : padded] - right) * w, 0.0)
        for at, part in ((0, left), (MARGIN, center), (MARGIN + width, right)):
            hi, lo = split(part)
            rhi[c, at : at + part.shape[0], :] = hi
            rlo[c, at : at + part.shape[0], :] = lo
        turned[c] = center.T
        res_ref[c] = turned[c, pl.ds(first_row, res_ref.shape[1]), :]

    for c in range(COMPS):
        for b in range(0, width // BLOCK, 2):
            rhs = stacked(rhi.at[c], rlo.at[c], [b, b + 1])
            out = jnp.dot(tb[128 * c : 128 * (c + 1), :], rhs, preferred_element_type=F32)
            hi, lo = split(out)
            for i, bb in enumerate((b, b + 1)):
                for r in range(RANK):
                    at = 128 * (RANK * c + r)
                    rows = slice(BLOCK * bb, BLOCK * (bb + 1))
                    bhi[rows, at : at + 128] = hi[BLOCK * r : BLOCK * (r + 1), 128 * i : 128 * (i + 1)]
                    blo[rows, at : at + 128] = lo[BLOCK * r : BLOCK * (r + 1), 128 * i : 128 * (i + 1)]
    out = jnp.dot(bhi[...], zb[...], preferred_element_type=F32)
    out = out + jnp.dot(blo[...], zb[...], preferred_element_type=F32)
    adjoint = (out[:, 0:128] + out[:, 128:256]).T
    grad_ref[0] = adjoint + PRIOR_WEIGHT * (jnp.log(dens[0][0]) - jnp.log(prior_ref[0]))


def compute(layers, share, dens, prior, observed, across, along, weight, e, o, eds, ods):
    rows, width = dens[0].shape[1:]
    padded = width + 2 * MARGIN
    vmem = pl.BlockSpec(memory_space=pltpu.VMEM)
    smem = pl.BlockSpec(memory_space=pltpu.SMEM)
    n_in = layers + 7 + 2 * (layers - 1)
    specs = [vmem] * n_in
    specs[layers + 4] = smem
    scratch = [
        pltpu.VMEM((layers, width + 2 * HALO, rows), BF16),
        pltpu.VMEM((layers, width + 2 * HALO, rows), BF16),
        pltpu.VMEM((layers, FILTERS * BLOCK, 256), BF16),
        pltpu.VMEM((COMPS, layers * RANK * rows, 256), BF16),
        pltpu.VMEM((FILTERS * BLOCK, 256), BF16),
        pltpu.VMEM((FILTERS * rows, 256), BF16),
        pltpu.VMEM((COMPS, padded, layers * RANK * rows), BF16),
        pltpu.VMEM((COMPS, padded, layers * RANK * rows), BF16),
        pltpu.VMEM((COMPS, padded, rows), BF16),
        pltpu.VMEM((COMPS, padded, rows), BF16),
        pltpu.VMEM((width, FILTERS * rows), BF16),
        pltpu.VMEM((width, FILTERS * rows), BF16),
        pltpu.VMEM((layers, 2, FILTERS, 128), F32),
        pltpu.VMEM((2, FILTERS, 128), F32),
        pltpu.VMEM((COMPS, rows, width), F32),
    ]
    return pl.pallas_call(
        lambda *refs: main_kernel(layers, *refs),
        out_shape=[
            jax.ShapeDtypeStruct((1, rows, width), F32),
            jax.ShapeDtypeStruct((COMPS, share, width), F32),
        ],
        in_specs=specs,
        out_specs=[vmem, vmem],
        scratch_shapes=scratch,
        compiler_params=pltpu.CompilerParams(vmem_limit_bytes=60 * 1024 * 1024),
        name="gradient",
    )(*dens, prior, observed, across, along, weight, e, o, *eds, *ods)


def body(density, prior, observed, filter_across, filter_along, comp_weight):
    layers, tiles = lax.axis_size("depth"), lax.axis_size("tile")
    share = density.shape[1] // layers
    both = ("depth", "tile")
    at = lambda d, t: d * tiles + t
    inner = [(i, i ^ 1) for i in range(tiles)]
    outer = [(i, i + 1) for i in range(1, tiles - 1, 2)] + [(i + 1, i) for i in range(1, tiles - 1, 2)]
    ends = lambda shift: [(at(d, t), at((d ^ 1) if shift == 0 else (d + shift) % layers, t)) for d in range(layers) for t in (0, tiles - 1)]
    hop = lambda pairs, s: [(at(d, i), at((d + s) % layers, j)) for d in range(layers) for i, j in pairs]
    dens = [density]
    for s in range(1, layers):
        dens.append(lax.ppermute(density, "depth", [(d, (d + s) % layers) for d in range(layers)]))
    e, o, ed, od = pack(density, observed, filter_across, filter_along)
    from_e = lax.ppermute(e, "tile", inner)
    from_o = lax.ppermute(o, both, hop(outer, 0) + ends(0))
    eds = [lax.ppermute(ed, both, hop(inner, s)) for s in range(1, layers)]
    ods = [lax.ppermute(od, both, hop(outer, s) + ends(s)) for s in range(1, layers)]
    return tuple(
        compute(layers, share, dens, prior, observed, filter_across, filter_along, comp_weight, from_e, from_o, eds, ods)
    )


def solution(mesh):
    placed = (
        P("depth", None, "tile"),
        P("depth", None, "tile"),
        P(None, None, "tile"),
        P("depth", None, None, None),
        P("depth", None, None, None),
        P(),
    )
    return jax.shard_map(
        body,
        mesh=mesh,
        in_specs=placed,
        out_specs=(P("depth", None, "tile"), P(None, "depth", "tile")),
        check_vma=False,
    )
```

```python
import jax
import jax.numpy as jnp
from jax import lax
from jax.experimental import pallas as pl
from jax.experimental.pallas import tpu as pltpu
from jax.sharding import PartitionSpec as P

COMPS = 6
RANK = 4
TAPS = 33
MARGIN = 16
HALO = 32
BLOCK = 32
LANES = 128
FILTERS = COMPS * RANK
ALONG_AT = 64
PRIOR_WEIGHT = 0.5
F32 = jnp.float32
BF16 = jnp.bfloat16
VMEM = pl.BlockSpec(memory_space=pltpu.VMEM)
HBM = pl.BlockSpec(memory_space=pltpu.HBM)
SMEM = pl.BlockSpec(memory_space=pltpu.SMEM)


def split(x):
    hi = x.astype(BF16)
    return hi, (x - hi.astype(F32)).astype(BF16)


def in_hbm(*arrays):
    return [pltpu.with_memory_space_constraint(x, pltpu.HBM) for x in arrays]


def limit(mib):
    return pltpu.CompilerParams(vmem_limit_bytes=mib << 20)


def pack_kernel(d_hbm, o_hbm, fa_hbm, fl_hbm, body_ref, e_ref, o_ref, d, o, fa, fl, sems):
    copies = [pltpu.make_async_copy(a, b, sems.at[i]) for i, (a, b) in enumerate(((d_hbm, d), (fa_hbm, fa), (fl_hbm, fl), (o_hbm, o)))]
    for copy in copies:
        copy.start()
    width = d.shape[2]
    even = lax.rem(lax.axis_index("tile"), 2) == 0
    for copy in copies[:3]:
        copy.wait()
    turned = d[0].T
    body_ref[0:width, :] = turned
    first, last = turned[0:HALO], turned[width - HALO : width]
    e_ref[0:HALO, :] = jnp.where(even, last, first)
    o_ref[0:HALO, :] = jnp.where(even, first, last)
    body_ref[width : width + FILTERS, :] = jnp.zeros((FILTERS, LANES), F32)
    for c in range(COMPS):
        rows = slice(width + RANK * c, width + RANK * (c + 1))
        body_ref[rows, 0:TAPS] = fa[0, c]
        body_ref[rows, ALONG_AT : ALONG_AT + TAPS] = fl[0, c]
    copies[3].wait()
    for c in range(COMPS):
        first = o[c, :, 0:LANES].T[0:MARGIN]
        last = o[c, :, width - LANES : width].T[LANES - MARGIN : LANES]
        rows = slice(HALO + MARGIN * c, HALO + MARGIN * (c + 1))
        e_ref[rows, :] = jnp.where(even, last, first)
        o_ref[rows, :] = jnp.where(even, first, last)


def pack(density, observed, across, along):
    width = density.shape[2]
    message = HALO + COMPS * MARGIN
    return pl.pallas_call(
        pack_kernel,
        out_shape=[
            jax.ShapeDtypeStruct((width + FILTERS, LANES), F32),
            jax.ShapeDtypeStruct((message, LANES), F32),
            jax.ShapeDtypeStruct((message, LANES), F32),
        ],
        in_specs=[HBM] * 4,
        out_specs=[VMEM] * 3,
        scratch_shapes=[pltpu.VMEM(x.shape, F32) for x in (density, observed, across, along)] + [pltpu.SemaphoreType.DMA((4,))],
        compiler_params=limit(8),
        name="pack",
    )(*in_hbm(density, observed, across, along))


def place(filters, first_tap, targets):
    tap = lax.broadcasted_iota(jnp.int32, (LANES, LANES), 0) - first_tap
    lane = lax.broadcasted_iota(jnp.int32, (LANES, LANES), 1)
    chosen = jnp.zeros((LANES, LANES), jnp.bool_)
    for target in targets(tap):
        chosen = chosen | (lane == target)
    chosen = (chosen & (tap >= 0) & (tap < TAPS)).astype(BF16)
    return [jnp.dot(v, chosen, preferred_element_type=F32) for v in split(filters)]


def along_blocks(base, filters, targets, dst):
    for p, placed in enumerate(place(filters, ALONG_AT, targets)):
        base[p] = placed
    for f in range(FILTERS):
        for p in range(2):
            v = jnp.broadcast_to(base[p, f : f + 1, :], (BLOCK, LANES))
            v = pltpu.roll(v, 0, 1, stride=1, stride_axis=0)
            dst[BLOCK * f : BLOCK * (f + 1), LANES * p : LANES * (p + 1)] = v.astype(BF16)


def across_blocks(base, filters, targets, dst):
    for p, placed in enumerate(place(filters, 0, targets)):
        base[p] = placed
    row = lax.broadcasted_iota(jnp.int32, (LANES, LANES), 0)
    lane = lax.broadcasted_iota(jnp.int32, (LANES, LANES), 1)
    band = jnp.abs(row - lane) <= MARGIN
    for f in range(FILTERS):
        for p in range(2):
            v = jnp.broadcast_to(base[p, f : f + 1, :], (LANES, LANES))
            v = pltpu.roll(v, 0, 1, stride=1, stride_axis=0)
            dst[LANES * f : LANES * (f + 1), LANES * p : LANES * (p + 1)] = jnp.where(band, v, 0.0).astype(BF16)


def forward_tables(base, filters, tf, zf):
    along_blocks(base, filters, lambda k: (k, k + 64), tf)
    across_blocks(base, filters, lambda k: ((MARGIN - k) & (LANES - 1),), zf)


def stacked(windows):
    columns = [jnp.concatenate([hi, lo, hi, lo], axis=0) for hi, lo in windows]
    return jnp.concatenate(columns, axis=1) if len(columns) > 1 else columns[0]


def smooth(table, windows, stores):
    hi, lo = split(jnp.dot(table, stacked(windows), preferred_element_type=F32))
    for i, store in enumerate(stores):
        for f in range(table.shape[0] // BLOCK):
            part = (slice(BLOCK * f, BLOCK * (f + 1)), slice(LANES * i, LANES * (i + 1)))
            store(f, hi[part], lo[part])


def into(shi, slo, row):
    def store(f, hi, lo):
        c, r = divmod(f, RANK)
        at = (c, slice(row, row + BLOCK), slice(LANES * r, LANES * (r + 1)))
        shi[at] = hi
        slo[at] = lo

    return store


def smooth_inside(body_ref, dhi, dlo, tf, shi, slo):
    width = dhi.shape[0]
    dhi[...], dlo[...] = split(body_ref[0:width, :])
    inside = width // BLOCK - 1
    window = lambda b: (dhi[BLOCK * b : BLOCK * b + 64, :], dlo[BLOCK * b : BLOCK * b + 64, :])
    for b in range(0, inside, 2):
        group = range(b, min(b + 2, inside))
        smooth(tf[...], [window(i) for i in group], [into(shi, slo, BLOCK * i) for i in group])


def own_kernel(body_ref, o_hbm, tf, zf, tb, zb, shi, slo, obst, dhi, dlo, base, o, sem):
    copy = pltpu.make_async_copy(o_hbm, o, sem)
    copy.start()
    width = dhi.shape[0]
    filters = body_ref[width : width + FILTERS, :]
    forward_tables(base, filters, tf, zf)
    smooth_inside(body_ref, dhi, dlo, tf, shi, slo)
    along_blocks(base, filters, lambda k: (TAPS - 1 - k, TAPS - 1 - k + 64), tb)
    across_blocks(base, filters, lambda k: ((k - MARGIN) & (LANES - 1),), zb)
    copy.wait()
    for c in range(COMPS):
        obst[c] = o[c].T


def other_kernel(body_ref, tf, zf, shi, slo, dhi, dlo, base):
    width = dhi.shape[0]
    forward_tables(base, body_ref[width : width + FILTERS, :], tf, zf)
    smooth_inside(body_ref, dhi, dlo, tf, shi, slo)


def tables(width):
    along = jax.ShapeDtypeStruct((FILTERS * BLOCK, 2 * LANES), BF16)
    across = jax.ShapeDtypeStruct((FILTERS * LANES, 2 * LANES), BF16)
    smoothed = jax.ShapeDtypeStruct((COMPS, width - BLOCK, RANK * LANES), BF16)
    scratch = [pltpu.VMEM((width, LANES), BF16)] * 2 + [pltpu.VMEM((2, FILTERS, LANES), F32)]
    return along, across, smoothed, scratch


def own_part(sent, observed):
    width = observed.shape[2]
    along, across, smoothed, scratch = tables(width)
    out = [along, across, along, across, smoothed, smoothed, jax.ShapeDtypeStruct((COMPS, width, LANES), F32)]
    return pl.pallas_call(
        own_kernel,
        out_shape=out,
        in_specs=[VMEM, HBM],
        out_specs=[VMEM] * len(out),
        scratch_shapes=scratch + [pltpu.VMEM(observed.shape, F32), pltpu.SemaphoreType.DMA],
        compiler_params=limit(8),
        cost_estimate=pl.CostEstimate(flops=2_000_000_000, bytes_accessed=4_000_000, transcendentals=0),
        name="own",
    )(sent, *in_hbm(observed))


def other_part(received):
    width = received.shape[0] - FILTERS
    along, across, smoothed, scratch = tables(width)
    return pl.pallas_call(
        other_kernel,
        out_shape=[along, across, smoothed, smoothed],
        in_specs=[VMEM],
        out_specs=[VMEM] * 4,
        scratch_shapes=scratch,
        compiler_params=limit(8),
        cost_estimate=pl.CostEstimate(flops=2_000_000_000, bytes_accessed=4_000_000, transcendentals=0),
        name="other",
    )(received)


def final_kernel(layers, *refs):
    it = iter(refs)
    take = lambda k: [next(it) for _ in range(k)]
    d_hbm, p_hbm, w_ref, e_ref, o_ref, tb, zb, obst = take(8)
    bodies, tfs, zfs, shis, slos = (take(layers) for _ in range(5))
    halos = take(layers - 1)
    grad_hbm, res_hbm = take(2)
    ehi, elo, rhi, rlo, bhi, blo, turned, res, d, p, grad, sems = take(12)
    copy_d = pltpu.make_async_copy(d_hbm, d, sems.at[0])
    copy_p = pltpu.make_async_copy(p_hbm, p, sems.at[1])
    copy_d.start()
    copy_p.start()
    tile, tiles = lax.axis_index("tile"), lax.axis_size("tile")
    even = lax.rem(tile, 2) == 0
    has_left, has_right = tile > 0, tile < tiles - 1
    width = obst.shape[1]
    share = res.shape[1]
    padded = width + 2 * MARGIN
    for l in range(layers):
        from_e = e_ref[0:HALO, :] if l == 0 else halos[l - 1][0:HALO, :]
        from_o = o_ref[0:HALO, :] if l == 0 else halos[l - 1][HALO : 2 * HALO, :]
        left = jnp.where(has_left, jnp.where(even, from_o, from_e), 0.0)
        right = jnp.where(has_right, jnp.where(even, from_e, from_o), 0.0)
        windows = [
            split(jnp.concatenate([left, bodies[l][0:HALO, :]], axis=0)),
            split(jnp.concatenate([bodies[l][width - HALO : width, :], right], axis=0)),
        ]
        smooth(tfs[l][...], windows, [into(ehi.at[l], elo.at[l], 0), into(ehi.at[l], elo.at[l], BLOCK)])

    first_row = lax.axis_index("depth") * share
    for c in range(COMPS):
        lhs, rhs = [], []
        for edge, inside in ((ehi, shis), (elo, slos)):
            for l in range(layers):
                lhs.append(jnp.concatenate([edge[l, c, 0:BLOCK, :], inside[l][c], edge[l, c, BLOCK : 2 * BLOCK, :]], axis=0))
                rhs.append(zfs[l][RANK * LANES * c : RANK * LANES * (c + 1), :])
        out = jnp.dot(jnp.concatenate(lhs, axis=1), jnp.concatenate(rhs, axis=0), preferred_element_type=F32)
        response = out[:, 0:LANES] + out[:, LANES : 2 * LANES]
        w = w_ref[c]
        center = (response[MARGIN : MARGIN + width] - obst[c]) * w
        rows = slice(HALO + MARGIN * c, HALO + MARGIN * (c + 1))
        left = jnp.where(even, o_ref[rows, :], e_ref[rows, :])
        right = jnp.where(even, e_ref[rows, :], o_ref[rows, :])
        left = jnp.where(has_left, (response[0:MARGIN] - left) * w, 0.0)
        right = jnp.where(has_right, (response[MARGIN + width : padded] - right) * w, 0.0)
        for at, part in ((0, left), (MARGIN, center), (MARGIN + width, right)):
            hi, lo = split(part)
            rhi[c, at : at + part.shape[0], :] = hi
            rlo[c, at : at + part.shape[0], :] = lo
        turned[c] = center.T
        res[c] = turned[c, pl.ds(first_row, share), :]
    copy_res = pltpu.make_async_copy(res, res_hbm, sems.at[2])
    copy_res.start()

    for c in range(COMPS):
        window = lambda b: (rhi[c, BLOCK * b : BLOCK * b + 64, :], rlo[c, BLOCK * b : BLOCK * b + 64, :])

        def store(b):
            def put(r, hi, lo):
                at = (slice(BLOCK * b, BLOCK * (b + 1)), slice(LANES * (RANK * c + r), LANES * (RANK * c + r + 1)))
                bhi[at] = hi
                blo[at] = lo

            return put

        table = tb[RANK * BLOCK * c : RANK * BLOCK * (c + 1), :]
        for b in range(0, width // BLOCK, 2):
            smooth(table, [window(b), window(b + 1)], [store(b), store(b + 1)])
    z = zb[...]
    out = jnp.dot(jnp.concatenate([bhi[...], blo[...]], axis=1), jnp.concatenate([z, z], axis=0), preferred_element_type=F32)
    adjoint = (out[:, 0:LANES] + out[:, LANES : 2 * LANES]).T
    copy_d.wait()
    copy_p.wait()
    grad[0] = adjoint + PRIOR_WEIGHT * (jnp.log(d[0]) - jnp.log(p[0]))
    copy_grad = pltpu.make_async_copy(grad, grad_hbm, sems.at[3])
    copy_grad.start()
    copy_res.wait()
    copy_grad.wait()


def final_part(layers, density, prior, weight, e, o, tb, zb, obst, bodies, tfs, zfs, shis, slos, halos):
    rows, width = density.shape[1:]
    share = rows // layers
    padded = width + 2 * MARGIN
    args = [*in_hbm(density, prior), weight, e, o, tb, zb, obst, *bodies, *tfs, *zfs, *shis, *slos, *halos]
    return pl.pallas_call(
        lambda *refs: final_kernel(layers, *refs),
        out_shape=[jax.ShapeDtypeStruct((1, rows, width), F32), jax.ShapeDtypeStruct((COMPS, share, width), F32)],
        in_specs=[HBM, HBM, SMEM] + [VMEM] * (len(args) - 3),
        out_specs=[HBM, HBM],
        scratch_shapes=[
            *[pltpu.VMEM((layers, COMPS, 2 * BLOCK, RANK * LANES), BF16)] * 2,
            *[pltpu.VMEM((COMPS, padded, LANES), BF16)] * 2,
            *[pltpu.VMEM((width, FILTERS * LANES), BF16)] * 2,
            pltpu.VMEM((COMPS, rows, width), F32),
            pltpu.VMEM((COMPS, share, width), F32),
            *[pltpu.VMEM((1, rows, width), F32)] * 3,
            pltpu.SemaphoreType.DMA((4,)),
        ],
        compiler_params=limit(12 + 2 * layers),
        name="final",
    )(*args)


def body(density, prior, observed, filter_across, filter_along, comp_weight):
    layers, tiles = lax.axis_size("depth"), lax.axis_size("tile")
    both = ("depth", "tile")
    at = lambda d, t: d * tiles + t
    inner = [(i, i ^ 1) for i in range(tiles)]
    outer = [(at(d, i), at(d, i + 1)) for d in range(layers) for i in range(1, tiles - 1, 2)]
    outer += [(j, i) for i, j in outer]
    outer += [(at(d, t), at(d ^ 1, t)) for d in range(layers) for t in (0, tiles - 1)]
    turns = [[(d, (d + s) % layers) for d in range(layers)] for s in range(1, layers)]

    sent, e, o = pack(density, observed, filter_across, filter_along)
    bodies = [sent] + [lax.ppermute(sent, "depth", turn) for turn in turns]
    from_e = lax.ppermute(e, "tile", inner)
    from_o = lax.ppermute(o, both, outer)
    tf, zf, tb, zb, shi, slo, obst = own_part(sent, observed)
    halo = jnp.concatenate([from_e[0:HALO], from_o[0:HALO]], axis=0)
    halo, _ = lax.optimization_barrier((halo, obst))
    halos = [lax.ppermute(halo, "depth", turn) for turn in turns]
    others = [other_part(received) for received in bodies[1:]]
    tfs, zfs, shis, slos = ([first] + [x[i] for x in others] for i, first in enumerate((tf, zf, shi, slo)))
    return tuple(
        final_part(layers, density, prior, comp_weight, from_e, from_o, tb, zb, obst, bodies, tfs, zfs, shis, slos, halos)
    )


def solution(mesh):
    placed = (
        P("depth", None, "tile"),
        P("depth", None, "tile"),
        P(None, None, "tile"),
        P("depth", None, None, None),
        P("depth", None, None, None),
        P(),
    )
    return jax.shard_map(
        body,
        mesh=mesh,
        in_specs=placed,
        out_specs=(P("depth", None, "tile"), P(None, "depth", "tile")),
        check_vma=False,
    )
```

```python
import jax
import jax.numpy as jnp
from jax import lax
from jax.experimental import pallas as pl
from jax.experimental.pallas import tpu as pltpu
from jax.sharding import PartitionSpec as P

COMPS = 6
RANK = 4
TAPS = 33
MARGIN = 16
HALO = 32
BLOCK = 32
LANES = 128
FILTERS = COMPS * RANK
ALONG_AT = 64
PRIOR_WEIGHT = 0.5
F32 = jnp.float32
BF16 = jnp.bfloat16
VMEM = pl.BlockSpec(memory_space=pltpu.VMEM)
HBM = pl.BlockSpec(memory_space=pltpu.HBM)
SMEM = pl.BlockSpec(memory_space=pltpu.SMEM)


def split(x):
    hi = x.astype(BF16)
    return hi, (x - hi.astype(F32)).astype(BF16)


def in_hbm(*arrays):
    return [pltpu.with_memory_space_constraint(x, pltpu.HBM) for x in arrays]


def limit(mib):
    return pltpu.CompilerParams(vmem_limit_bytes=mib << 20)


def turn_kernel(d_hbm, fa_hbm, fl_hbm, o_hbm, body_ref, o_ref, d, fa, fl, sems):
    moves = ((fa_hbm, fa), (fl_hbm, fl), (d_hbm, d), (o_hbm, o_ref))
    copies = [pltpu.make_async_copy(a, b, sems.at[i]) for i, (a, b) in enumerate(moves)]
    for copy in copies:
        copy.start()
    for copy in copies[:3]:
        copy.wait()
    width = d.shape[2]
    body_ref[0:width, :] = d[0].T
    body_ref[width : width + FILTERS, :] = jnp.zeros((FILTERS, LANES), F32)
    for c in range(COMPS):
        rows = slice(width + RANK * c, width + RANK * (c + 1))
        body_ref[rows, 0:TAPS] = fa[0, c]
        body_ref[rows, ALONG_AT : ALONG_AT + TAPS] = fl[0, c]
    copies[3].wait()


def turn(density, across, along, observed):
    return pl.pallas_call(
        turn_kernel,
        out_shape=[
            jax.ShapeDtypeStruct((density.shape[2] + FILTERS, LANES), F32),
            jax.ShapeDtypeStruct(observed.shape, F32),
        ],
        in_specs=[HBM] * 4,
        out_specs=[VMEM] * 2,
        scratch_shapes=[pltpu.VMEM(x.shape, F32) for x in (density, across, along)] + [pltpu.SemaphoreType.DMA((4,))],
        compiler_params=limit(4),
        name="turn",
    )(*in_hbm(density, across, along, observed))


def is_even():
    return lax.rem(lax.axis_index("tile"), 2) == 0


def outer_edge(x):
    return jnp.where(is_even(), x[0:HALO, :], x[x.shape[0] - HALO : x.shape[0], :])


def inner_edge(x):
    return jnp.where(is_even(), x[x.shape[0] - HALO : x.shape[0], :], x[0:HALO, :])


def outer_kernel(body_ref, o_ref, out_ref, od_ref, in_ref):
    width = o_ref.shape[2]
    even = is_even()
    edge = outer_edge(body_ref.at[0:width])
    out_ref[0:HALO, :] = edge
    od_ref[...] = edge
    for c in range(COMPS):
        first = o_ref[c, :, 0:LANES].T[0:MARGIN]
        last = o_ref[c, :, width - LANES : width].T[LANES - MARGIN : LANES]
        out_ref[HALO + MARGIN * c : HALO + MARGIN * (c + 1), :] = jnp.where(even, first, last)
        in_ref[MARGIN * c : MARGIN * (c + 1), :] = jnp.where(even, last, first)


def outer_part(sent, observed):
    return pl.pallas_call(
        outer_kernel,
        out_shape=[
            jax.ShapeDtypeStruct((HALO + COMPS * MARGIN, LANES), F32),
            jax.ShapeDtypeStruct((HALO, LANES), F32),
            jax.ShapeDtypeStruct((COMPS * MARGIN, LANES), F32),
        ],
        in_specs=[VMEM] * 2,
        out_specs=[VMEM] * 3,
        compiler_params=limit(4),
        name="outer",
    )(sent, observed)


def inner_kernel(layers, *refs):
    obs_ref, bodies, out_ref = refs[0], refs[1:-1], refs[-1]
    width = bodies[0].shape[0] - FILTERS
    for l in range(layers):
        out_ref[HALO * l : HALO * (l + 1), :] = inner_edge(bodies[l].at[0:width])
    out_ref[HALO * layers :, :] = obs_ref[...]


def inner_part(edge, bodies):
    layers = len(bodies)
    return pl.pallas_call(
        lambda *refs: inner_kernel(layers, *refs),
        out_shape=jax.ShapeDtypeStruct((HALO * layers + COMPS * MARGIN, LANES), F32),
        in_specs=[VMEM] * (1 + layers),
        out_specs=VMEM,
        compiler_params=limit(4),
        name="inner",
    )(edge, *bodies)


def place(filters, first_tap, targets):
    tap = lax.broadcasted_iota(jnp.int32, (LANES, LANES), 0) - first_tap
    lane = lax.broadcasted_iota(jnp.int32, (LANES, LANES), 1)
    chosen = jnp.zeros((LANES, LANES), jnp.bool_)
    for target in targets(tap):
        chosen = chosen | (lane == target)
    chosen = (chosen & (tap >= 0) & (tap < TAPS)).astype(BF16)
    return [jnp.dot(v, chosen, preferred_element_type=F32) for v in split(filters)]


def along_blocks(base, filters, targets, dst):
    for p, placed in enumerate(place(filters, ALONG_AT, targets)):
        base[p] = placed
    for f in range(FILTERS):
        for p in range(2):
            v = jnp.broadcast_to(base[p, f : f + 1, :], (BLOCK, LANES))
            v = pltpu.roll(v, 0, 1, stride=1, stride_axis=0)
            dst[BLOCK * f : BLOCK * (f + 1), LANES * p : LANES * (p + 1)] = v.astype(BF16)


def across_blocks(base, filters, targets, dst):
    for p, placed in enumerate(place(filters, 0, targets)):
        base[p] = placed
    row = lax.broadcasted_iota(jnp.int32, (LANES, LANES), 0)
    lane = lax.broadcasted_iota(jnp.int32, (LANES, LANES), 1)
    band = jnp.abs(row - lane) <= MARGIN
    for f in range(FILTERS):
        for p in range(2):
            v = jnp.broadcast_to(base[p, f : f + 1, :], (LANES, LANES))
            v = pltpu.roll(v, 0, 1, stride=1, stride_axis=0)
            dst[LANES * f : LANES * (f + 1), LANES * p : LANES * (p + 1)] = jnp.where(band, v, 0.0).astype(BF16)


def forward_tables(base, filters, tf, zf):
    along_blocks(base, filters, lambda k: (k, k + 64), tf)
    across_blocks(base, filters, lambda k: ((MARGIN - k) & (LANES - 1),), zf)


def stacked(windows):
    columns = [jnp.concatenate([hi, lo, hi, lo], axis=0) for hi, lo in windows]
    return jnp.concatenate(columns, axis=1) if len(columns) > 1 else columns[0]


def smooth(table, windows, stores):
    hi, lo = split(jnp.dot(table, stacked(windows), preferred_element_type=F32))
    for i, store in enumerate(stores):
        for f in range(table.shape[0] // BLOCK):
            part = (slice(BLOCK * f, BLOCK * (f + 1)), slice(LANES * i, LANES * (i + 1)))
            store(f, hi[part], lo[part])


def into(shi, slo, row):
    def store(f, hi, lo):
        c, r = divmod(f, RANK)
        at = (c, slice(row, row + BLOCK), slice(LANES * r, LANES * (r + 1)))
        shi[at] = hi
        slo[at] = lo

    return store


def smooth_inside(body_ref, dhi, dlo, tf, shi, slo):
    width = dhi.shape[0]
    dhi[...], dlo[...] = split(body_ref[0:width, :])
    inside = width // BLOCK - 1
    window = lambda b: (dhi[BLOCK * b : BLOCK * b + 64, :], dlo[BLOCK * b : BLOCK * b + 64, :])
    for b in range(0, inside, 2):
        group = range(b, min(b + 2, inside))
        smooth(tf[...], [window(i) for i in group], [into(shi, slo, BLOCK * i) for i in group])


def own_kernel(body_ref, o_ref, tf, zf, tb, zb, shi, slo, obst, dhi, dlo, base):
    width = dhi.shape[0]
    filters = body_ref[width : width + FILTERS, :]
    forward_tables(base, filters, tf, zf)
    smooth_inside(body_ref, dhi, dlo, tf, shi, slo)
    along_blocks(base, filters, lambda k: (TAPS - 1 - k, TAPS - 1 - k + 64), tb)
    across_blocks(base, filters, lambda k: ((k - MARGIN) & (LANES - 1),), zb)
    for c in range(COMPS):
        obst[c] = o_ref[c].T


def other_kernel(body_ref, tf, zf, shi, slo, dhi, dlo, base):
    width = dhi.shape[0]
    forward_tables(base, body_ref[width : width + FILTERS, :], tf, zf)
    smooth_inside(body_ref, dhi, dlo, tf, shi, slo)


def tables(width):
    along = jax.ShapeDtypeStruct((FILTERS * BLOCK, 2 * LANES), BF16)
    across = jax.ShapeDtypeStruct((FILTERS * LANES, 2 * LANES), BF16)
    smoothed = jax.ShapeDtypeStruct((COMPS, width - BLOCK, RANK * LANES), BF16)
    scratch = [pltpu.VMEM((width, LANES), BF16)] * 2 + [pltpu.VMEM((2, FILTERS, LANES), F32)]
    return along, across, smoothed, scratch


def own_part(sent, observed):
    width = observed.shape[2]
    along, across, smoothed, scratch = tables(width)
    out = [along, across, along, across, smoothed, smoothed, jax.ShapeDtypeStruct((COMPS, width, LANES), F32)]
    return pl.pallas_call(
        own_kernel,
        out_shape=out,
        in_specs=[VMEM, VMEM],
        out_specs=[VMEM] * len(out),
        scratch_shapes=scratch,
        compiler_params=limit(8),
        cost_estimate=pl.CostEstimate(flops=2_000_000_000, bytes_accessed=4_000_000, transcendentals=0),
        name="own",
    )(sent, observed)


def other_part(received):
    width = received.shape[0] - FILTERS
    along, across, smoothed, scratch = tables(width)
    return pl.pallas_call(
        other_kernel,
        out_shape=[along, across, smoothed, smoothed],
        in_specs=[VMEM],
        out_specs=[VMEM] * 4,
        scratch_shapes=scratch,
        compiler_params=limit(8),
        cost_estimate=pl.CostEstimate(flops=2_000_000_000, bytes_accessed=4_000_000, transcendentals=0),
        name="other",
    )(received)


def final_kernel(layers, *refs):
    it = iter(refs)
    take = lambda k: [next(it) for _ in range(k)]
    d_hbm, p_hbm, w_ref, e_ref, o_ref, tb, zb, obst = take(8)
    bodies, tfs, zfs, shis, slos = (take(layers) for _ in range(5))
    halos = take(layers - 1)
    grad_hbm, res_hbm = take(2)
    ehi, elo, rhi, rlo, bhi, blo, turned, res, d, p, grad, acc, sems = take(13)
    copy_d = pltpu.make_async_copy(d_hbm, d, sems.at[0])
    copy_p = pltpu.make_async_copy(p_hbm, p, sems.at[1])
    copy_d.start()
    copy_p.start()
    tile, tiles = lax.axis_index("tile"), lax.axis_size("tile")
    even = is_even()
    has_left, has_right = tile > 0, tile < tiles - 1
    width = obst.shape[1]
    share = res.shape[1]
    padded = width + 2 * MARGIN
    for l in range(layers):
        from_e = e_ref[HALO * l : HALO * (l + 1), :]
        from_o = o_ref[0:HALO, :] if l == 0 else halos[l - 1][...]
        left = jnp.where(has_left, jnp.where(even, from_o, from_e), 0.0)
        right = jnp.where(has_right, jnp.where(even, from_e, from_o), 0.0)
        windows = [
            split(jnp.concatenate([left, bodies[l][0:HALO, :]], axis=0)),
            split(jnp.concatenate([bodies[l][width - HALO : width, :], right], axis=0)),
        ]
        smooth(tfs[l][...], windows, [into(ehi.at[l], elo.at[l], 0), into(ehi.at[l], elo.at[l], BLOCK)])

    first_row = lax.axis_index("depth") * share

    def forward(c):
        lhs, rhs = [], []
        for edge, inside in ((ehi, shis), (elo, slos)):
            for l in range(layers):
                lhs.append(jnp.concatenate([edge[l, c, 0:BLOCK, :], inside[l][c], edge[l, c, BLOCK : 2 * BLOCK, :]], axis=0))
                rhs.append(zfs[l][RANK * LANES * c : RANK * LANES * (c + 1), :])
        out = jnp.dot(jnp.concatenate(lhs, axis=1), jnp.concatenate(rhs, axis=0), preferred_element_type=F32)
        response = out[:, 0:LANES] + out[:, LANES : 2 * LANES]
        w = w_ref[c]
        center = (response[MARGIN : MARGIN + width] - obst[c]) * w
        from_o = o_ref[HALO + MARGIN * c : HALO + MARGIN * (c + 1), :]
        from_e = e_ref[HALO * layers + MARGIN * c : HALO * layers + MARGIN * (c + 1), :]
        left = jnp.where(even, from_o, from_e)
        right = jnp.where(even, from_e, from_o)
        left = jnp.where(has_left, (response[0:MARGIN] - left) * w, 0.0)
        right = jnp.where(has_right, (response[MARGIN + width : padded] - right) * w, 0.0)
        for at, part in ((0, left), (MARGIN, center), (MARGIN + width, right)):
            hi, lo = split(part)
            rhi[c, at : at + part.shape[0], :] = hi
            rlo[c, at : at + part.shape[0], :] = lo
        turned[c] = center.T
        res[c] = turned[c, pl.ds(first_row, share), :]

    def adjoint(c):
        window = lambda b: (rhi[c, BLOCK * b : BLOCK * b + 64, :], rlo[c, BLOCK * b : BLOCK * b + 64, :])

        def store(b):
            def put(r, hi, lo):
                at = (c, slice(BLOCK * b, BLOCK * (b + 1)), slice(LANES * r, LANES * (r + 1)))
                bhi[at] = hi
                blo[at] = lo

            return put

        table = tb[RANK * BLOCK * c : RANK * BLOCK * (c + 1), :]
        for b in range(0, width // BLOCK, 2):
            smooth(table, [window(b), window(b + 1)], [store(b), store(b + 1)])
        z = zb[RANK * LANES * c : RANK * LANES * (c + 1), :]
        return jnp.dot(jnp.concatenate([bhi[c], blo[c]], axis=1), jnp.concatenate([z, z], axis=0), preferred_element_type=F32)

    for c in range(COMPS + 1):
        if c < COMPS:
            forward(c)
        if c == COMPS - 1:
            copy_res = pltpu.make_async_copy(res, res_hbm, sems.at[2])
            copy_res.start()
        if c == 1:
            acc[...] = adjoint(0)
        if c > 1:
            acc[...] += adjoint(c - 1)
    out = acc[...]
    adj = (out[:, 0:LANES] + out[:, LANES : 2 * LANES]).T
    copy_d.wait()
    copy_p.wait()
    grad[0] = adj + PRIOR_WEIGHT * (jnp.log(d[0]) - jnp.log(p[0]))
    copy_grad = pltpu.make_async_copy(grad, grad_hbm, sems.at[3])
    copy_grad.start()
    copy_res.wait()
    copy_grad.wait()


def final_part(layers, density, prior, weight, e, o, tb, zb, obst, bodies, tfs, zfs, shis, slos, halos):
    rows, width = density.shape[1:]
    share = rows // layers
    padded = width + 2 * MARGIN
    args = [*in_hbm(density, prior), weight, e, o, tb, zb, obst, *bodies, *tfs, *zfs, *shis, *slos, *halos]
    return pl.pallas_call(
        lambda *refs: final_kernel(layers, *refs),
        out_shape=[jax.ShapeDtypeStruct((1, rows, width), F32), jax.ShapeDtypeStruct((COMPS, share, width), F32)],
        in_specs=[HBM, HBM, SMEM] + [VMEM] * (len(args) - 3),
        out_specs=[HBM, HBM],
        scratch_shapes=[
            *[pltpu.VMEM((layers, COMPS, 2 * BLOCK, RANK * LANES), BF16)] * 2,
            *[pltpu.VMEM((COMPS, padded, LANES), BF16)] * 2,
            *[pltpu.VMEM((COMPS, width, RANK * LANES), BF16)] * 2,
            pltpu.VMEM((COMPS, rows, width), F32),
            pltpu.VMEM((COMPS, share, width), F32),
            *[pltpu.VMEM((1, rows, width), F32)] * 3,
            pltpu.VMEM((width, 2 * LANES), F32),
            pltpu.SemaphoreType.DMA((4,)),
        ],
        compiler_params=limit(12 + 2 * layers),
        name="final",
    )(*args)


def body(density, prior, observed, filter_across, filter_along, comp_weight):
    layers, tiles = lax.axis_size("depth"), lax.axis_size("tile")
    both = ("depth", "tile")
    turns = [[(d, (d + s) % layers) for d in range(layers)] for s in range(layers)]
    inner = [(i, i ^ 1) for i in range(tiles)]
    outer = [(i, i + 1) for i in range(1, tiles - 1, 2)]
    outer += [(j, i) for i, j in outer]

    def outward(s):
        pairs = [(d * tiles + i, e * tiles + j) for d, e in turns[s] for i, j in outer]
        return pairs + [(d * tiles + t, (e if s else d ^ 1) * tiles + t) for d, e in turns[s] for t in (0, tiles - 1)]

    sent, observed = turn(density, filter_across, filter_along, observed)
    bodies = [sent] + [lax.ppermute(sent, "depth", pairs) for pairs in turns[1:]]
    out, out_other, inside = outer_part(sent, observed)
    from_o = lax.ppermute(out, both, outward(0))
    halos = [lax.ppermute(out_other, both, outward(s)) for s in range(1, layers)]
    tf, zf, tb, zb, shi, slo, obst = own_part(sent, observed)
    inside, _ = lax.optimization_barrier((inside, obst))
    from_e = lax.ppermute(inner_part(inside, bodies), "tile", inner)
    others = [other_part(received) for received in bodies[1:]]
    tfs, zfs, shis, slos = ([first] + [x[i] for x in others] for i, first in enumerate((tf, zf, shi, slo)))
    return tuple(
        final_part(layers, density, prior, comp_weight, from_e, from_o, tb, zb, obst, bodies, tfs, zfs, shis, slos, halos)
    )


def solution(mesh):
    placed = (
        P("depth", None, "tile"),
        P("depth", None, "tile"),
        P(None, None, "tile"),
        P("depth", None, None, None),
        P("depth", None, None, None),
        P(),
    )
    return jax.shard_map(
        body,
        mesh=mesh,
        in_specs=placed,
        out_specs=(P("depth", None, "tile"), P(None, "depth", "tile")),
        check_vma=False,
    )
```

```python
import jax
import jax.numpy as jnp
from jax import lax
from jax.experimental import pallas as pl
from jax.experimental.pallas import tpu as pltpu
from jax.sharding import PartitionSpec as P

COMPS = 6
RANK = 4
TAPS = 33
MARGIN = 16
HALO = 32
BLOCK = 32
LANES = 128
FILTERS = COMPS * RANK
ALONG_AT = 64
PRIOR_WEIGHT = 0.5
F32 = jnp.float32
BF16 = jnp.bfloat16
VMEM = pl.BlockSpec(memory_space=pltpu.VMEM)
HBM = pl.BlockSpec(memory_space=pltpu.HBM)


def split(x):
    hi = x.astype(BF16)
    return hi, (x - hi.astype(F32)).astype(BF16)


def in_hbm(*arrays):
    return [pltpu.with_memory_space_constraint(x, pltpu.HBM) for x in arrays]


def limit(mib):
    return pltpu.CompilerParams(vmem_limit_bytes=mib << 20)


def turn_kernel(d_hbm, fa_hbm, fl_hbm, o_hbm, body_ref, o_ref, d, fa, fl, sems):
    moves = ((fa_hbm, fa), (fl_hbm, fl), (d_hbm, d), (o_hbm, o_ref))
    copies = [pltpu.make_async_copy(a, b, sems.at[i]) for i, (a, b) in enumerate(moves)]
    for copy in copies:
        copy.start()
    for copy in copies[:3]:
        copy.wait()
    width = d.shape[2]
    body_ref[0:width, :] = d[0].T
    body_ref[width : width + FILTERS, :] = jnp.zeros((FILTERS, LANES), F32)
    for c in range(COMPS):
        rows = slice(width + RANK * c, width + RANK * (c + 1))
        body_ref[rows, 0:TAPS] = fa[0, c]
        body_ref[rows, ALONG_AT : ALONG_AT + TAPS] = fl[0, c]
    copies[3].wait()


def turn(density, across, along, observed):
    return pl.pallas_call(
        turn_kernel,
        out_shape=[
            jax.ShapeDtypeStruct((density.shape[2] + FILTERS, LANES), F32),
            jax.ShapeDtypeStruct(observed.shape, F32),
        ],
        in_specs=[HBM] * 4,
        out_specs=[VMEM] * 2,
        scratch_shapes=[pltpu.VMEM(x.shape, F32) for x in (density, across, along)] + [pltpu.SemaphoreType.DMA((4,))],
        compiler_params=limit(4),
        name="turn",
    )(*in_hbm(density, across, along, observed))


def is_even():
    return lax.rem(lax.axis_index("tile"), 2) == 0


def outer_edge(x):
    return jnp.where(is_even(), x[0:HALO, :], x[x.shape[0] - HALO : x.shape[0], :])


def inner_edge(x):
    return jnp.where(is_even(), x[x.shape[0] - HALO : x.shape[0], :], x[0:HALO, :])


def outer_kernel(body_ref, o_ref, out_ref, od_ref, in_ref):
    width = o_ref.shape[2]
    even = is_even()
    edge = outer_edge(body_ref.at[0:width])
    out_ref[0:HALO, :] = edge
    od_ref[...] = edge
    for c in range(COMPS):
        first = o_ref[c, :, 0:LANES].T[0:MARGIN]
        last = o_ref[c, :, width - LANES : width].T[LANES - MARGIN : LANES]
        out_ref[HALO + MARGIN * c : HALO + MARGIN * (c + 1), :] = jnp.where(even, first, last)
        in_ref[MARGIN * c : MARGIN * (c + 1), :] = jnp.where(even, last, first)


def outer_part(sent, observed):
    return pl.pallas_call(
        outer_kernel,
        out_shape=[
            jax.ShapeDtypeStruct((HALO + COMPS * MARGIN, LANES), F32),
            jax.ShapeDtypeStruct((HALO, LANES), F32),
            jax.ShapeDtypeStruct((COMPS * MARGIN, LANES), F32),
        ],
        in_specs=[VMEM] * 2,
        out_specs=[VMEM] * 3,
        compiler_params=limit(4),
        name="outer",
    )(sent, observed)


def inner_kernel(layers, *refs):
    obs_ref, bodies, out_ref = refs[0], refs[1:-1], refs[-1]
    width = bodies[0].shape[0] - FILTERS
    for l in range(layers):
        out_ref[HALO * l : HALO * (l + 1), :] = inner_edge(bodies[l].at[0:width])
    out_ref[HALO * layers :, :] = obs_ref[...]


def inner_part(edge, bodies):
    layers = len(bodies)
    return pl.pallas_call(
        lambda *refs: inner_kernel(layers, *refs),
        out_shape=jax.ShapeDtypeStruct((HALO * layers + COMPS * MARGIN, LANES), F32),
        in_specs=[VMEM] * (1 + layers),
        out_specs=VMEM,
        compiler_params=limit(4),
        name="inner",
    )(edge, *bodies)


def place(base, filters, first_tap, targets):
    tap = lax.broadcasted_iota(jnp.int32, (LANES, LANES), 0) - first_tap
    lane = lax.broadcasted_iota(jnp.int32, (LANES, LANES), 1)
    chosen = jnp.zeros((LANES, LANES), jnp.bool_)
    for target in targets(tap):
        chosen = chosen | (lane == target)
    chosen = (chosen & (tap >= 0) & (tap < TAPS)).astype(BF16)
    hi, lo = (jnp.dot(v, chosen, preferred_element_type=F32) for v in split(filters))
    base[...] = hi + lo


def along_blocks(base, dst):
    for f in range(FILTERS):
        v = jnp.broadcast_to(base[f : f + 1, :], (BLOCK, LANES))
        v = pltpu.roll(v, 0, 1, stride=1, stride_axis=0)
        for p, part in enumerate(split(v)):
            dst[BLOCK * f : BLOCK * (f + 1), LANES * p : LANES * (p + 1)] = part


def across_blocks(base, dst):
    row = lax.broadcasted_iota(jnp.int32, (LANES, LANES), 0)
    lane = lax.broadcasted_iota(jnp.int32, (LANES, LANES), 1)
    band = jnp.abs(row - lane) <= MARGIN
    for f in range(FILTERS):
        v = jnp.broadcast_to(base[f : f + 1, :], (LANES, LANES))
        v = jnp.where(band, pltpu.roll(v, 0, 1, stride=1, stride_axis=0), 0.0)
        for p, part in enumerate(split(v)):
            dst[LANES * f : LANES * (f + 1), LANES * p : LANES * (p + 1)] = part


def forward_places(base, filters):
    place(base.at[0], filters, ALONG_AT, lambda k: (k, k + 64))
    place(base.at[1], filters, 0, lambda k: ((MARGIN - k) & (LANES - 1),))


def backward_places(base, filters):
    place(base.at[2], filters, ALONG_AT, lambda k: (TAPS - 1 - k, TAPS - 1 - k + 64))
    place(base.at[3], filters, 0, lambda k: ((k - MARGIN) & (LANES - 1),))


def stacked(windows):
    columns = [jnp.concatenate([hi, lo, hi, lo], axis=0) for hi, lo in windows]
    return jnp.concatenate(columns, axis=1) if len(columns) > 1 else columns[0]


def smooth(table, windows, stores):
    hi, lo = split(jnp.dot(table, stacked(windows), preferred_element_type=F32))
    for i, store in enumerate(stores):
        for f in range(table.shape[0] // BLOCK):
            part = (slice(BLOCK * f, BLOCK * (f + 1)), slice(LANES * i, LANES * (i + 1)))
            store(f, hi[part], lo[part])


def into(shi, slo, row):
    def store(f, hi, lo):
        c, r = divmod(f, RANK)
        at = (c, slice(row, row + BLOCK), slice(LANES * r, LANES * (r + 1)))
        shi[at] = hi
        slo[at] = lo

    return store


def smooth_inside(body_ref, dhi, dlo, tf, shi, slo):
    width = dhi.shape[0]
    dhi[...], dlo[...] = split(body_ref[0:width, :])
    inside = width // BLOCK - 1
    window = lambda b: (dhi[BLOCK * b : BLOCK * b + 64, :], dlo[BLOCK * b : BLOCK * b + 64, :])
    for b in range(0, inside, 2):
        group = range(b, min(b + 2, inside))
        smooth(tf[...], [window(i) for i in group], [into(shi, slo, BLOCK * i) for i in group])


def own_kernel(body_ref, o_ref, tf, zf, tb, zb, shi, slo, obst, dhi, dlo, base):
    width = dhi.shape[0]
    filters = body_ref[width : width + FILTERS, :]
    forward_places(base, filters)
    backward_places(base, filters)
    along_blocks(base.at[0], tf)
    smooth_inside(body_ref, dhi, dlo, tf, shi, slo)
    across_blocks(base.at[1], zf)
    along_blocks(base.at[2], tb)
    across_blocks(base.at[3], zb)
    for c in range(COMPS):
        obst[c] = o_ref[c].T


def other_kernel(body_ref, tf, zf, shi, slo, dhi, dlo, base):
    width = dhi.shape[0]
    forward_places(base, body_ref[width : width + FILTERS, :])
    along_blocks(base.at[0], tf)
    smooth_inside(body_ref, dhi, dlo, tf, shi, slo)
    across_blocks(base.at[1], zf)


def tables(width):
    along = jax.ShapeDtypeStruct((FILTERS * BLOCK, 2 * LANES), BF16)
    across = jax.ShapeDtypeStruct((FILTERS * LANES, 2 * LANES), BF16)
    smoothed = jax.ShapeDtypeStruct((COMPS, width - BLOCK, RANK * LANES), BF16)
    scratch = [pltpu.VMEM((width, LANES), BF16)] * 2 + [pltpu.VMEM((4, FILTERS, LANES), F32)]
    return along, across, smoothed, scratch


def own_part(sent, observed):
    width = observed.shape[2]
    along, across, smoothed, scratch = tables(width)
    out = [along, across, along, across, smoothed, smoothed, jax.ShapeDtypeStruct((COMPS, width, LANES), F32)]
    return pl.pallas_call(
        own_kernel,
        out_shape=out,
        in_specs=[VMEM, VMEM],
        out_specs=[VMEM] * len(out),
        scratch_shapes=scratch,
        compiler_params=limit(8),
        cost_estimate=pl.CostEstimate(flops=2_000_000_000, bytes_accessed=4_000_000, transcendentals=0),
        name="own",
    )(sent, observed)


def other_part(received):
    width = received.shape[0] - FILTERS
    along, across, smoothed, scratch = tables(width)
    return pl.pallas_call(
        other_kernel,
        out_shape=[along, across, smoothed, smoothed],
        in_specs=[VMEM],
        out_specs=[VMEM] * 4,
        scratch_shapes=scratch,
        compiler_params=limit(8),
        cost_estimate=pl.CostEstimate(flops=2_000_000_000, bytes_accessed=4_000_000, transcendentals=0),
        name="other",
    )(received)


def final_kernel(layers, *refs):
    it = iter(refs)
    take = lambda k: [next(it) for _ in range(k)]
    d_hbm, p_hbm, w_hbm, e_ref, o_ref, tb, zb, obst = take(8)
    bodies, tfs, zfs, shis, slos = (take(layers) for _ in range(5))
    halos = take(layers - 1)
    grad_hbm, res_hbm = take(2)
    ehi, elo, rhi, rlo, bhi, blo, turned, res, d, p, grad, acc, w_ref, sems = take(14)
    copy_d = pltpu.make_async_copy(d_hbm, d, sems.at[0])
    copy_p = pltpu.make_async_copy(p_hbm, p, sems.at[1])
    copy_w = pltpu.make_async_copy(w_hbm, w_ref, sems.at[4])
    copy_w.start()
    copy_d.start()
    copy_p.start()
    tile, tiles = lax.axis_index("tile"), lax.axis_size("tile")
    even = is_even()
    has_left, has_right = tile > 0, tile < tiles - 1
    width = obst.shape[1]
    share = res.shape[1]
    padded = width + 2 * MARGIN
    for l in range(layers):
        from_e = e_ref[HALO * l : HALO * (l + 1), :]
        from_o = o_ref[0:HALO, :] if l == 0 else halos[l - 1][...]
        left = jnp.where(has_left, jnp.where(even, from_o, from_e), 0.0)
        right = jnp.where(has_right, jnp.where(even, from_e, from_o), 0.0)
        windows = [
            split(jnp.concatenate([left, bodies[l][0:HALO, :]], axis=0)),
            split(jnp.concatenate([bodies[l][width - HALO : width, :], right], axis=0)),
        ]
        smooth(tfs[l][...], windows, [into(ehi.at[l], elo.at[l], 0), into(ehi.at[l], elo.at[l], BLOCK)])

    first_row = lax.axis_index("depth") * share
    copy_w.wait()

    def forward(c):
        lhs, rhs = [], []
        for edge, inside in ((ehi, shis), (elo, slos)):
            for l in range(layers):
                lhs.append(jnp.concatenate([edge[l, c, 0:BLOCK, :], inside[l][c], edge[l, c, BLOCK : 2 * BLOCK, :]], axis=0))
                rhs.append(zfs[l][RANK * LANES * c : RANK * LANES * (c + 1), :])
        out = jnp.dot(jnp.concatenate(lhs, axis=1), jnp.concatenate(rhs, axis=0), preferred_element_type=F32)
        response = out[:, 0:LANES] + out[:, LANES : 2 * LANES]
        w = w_ref[c]
        center = (response[MARGIN : MARGIN + width] - obst[c]) * w
        from_o = o_ref[HALO + MARGIN * c : HALO + MARGIN * (c + 1), :]
        from_e = e_ref[HALO * layers + MARGIN * c : HALO * layers + MARGIN * (c + 1), :]
        left = jnp.where(even, from_o, from_e)
        right = jnp.where(even, from_e, from_o)
        left = jnp.where(has_left, (response[0:MARGIN] - left) * w, 0.0)
        right = jnp.where(has_right, (response[MARGIN + width : padded] - right) * w, 0.0)
        for at, part in ((0, left), (MARGIN, center), (MARGIN + width, right)):
            hi, lo = split(part)
            rhi[c, at : at + part.shape[0], :] = hi
            rlo[c, at : at + part.shape[0], :] = lo
        turned[c] = center.T
        res[c] = turned[c, pl.ds(first_row, share), :]

    def adjoint(c):
        window = lambda b: (rhi[c, BLOCK * b : BLOCK * b + 64, :], rlo[c, BLOCK * b : BLOCK * b + 64, :])

        def store(b):
            def put(r, hi, lo):
                at = (c, slice(BLOCK * b, BLOCK * (b + 1)), slice(LANES * r, LANES * (r + 1)))
                bhi[at] = hi
                blo[at] = lo

            return put

        table = tb[RANK * BLOCK * c : RANK * BLOCK * (c + 1), :]
        for b in range(0, width // BLOCK, 2):
            smooth(table, [window(b), window(b + 1)], [store(b), store(b + 1)])
        z = zb[RANK * LANES * c : RANK * LANES * (c + 1), :]
        return jnp.dot(jnp.concatenate([bhi[c], blo[c]], axis=1), jnp.concatenate([z, z], axis=0), preferred_element_type=F32)

    for c in range(COMPS + 1):
        if c < COMPS:
            forward(c)
        if c == COMPS - 1:
            copy_res = pltpu.make_async_copy(res, res_hbm, sems.at[2])
            copy_res.start()
        if c == 1:
            acc[...] = adjoint(0)
        if c > 1:
            acc[...] += adjoint(c - 1)
    out = acc[...]
    adj = (out[:, 0:LANES] + out[:, LANES : 2 * LANES]).T
    copy_d.wait()
    copy_p.wait()
    grad[0] = adj + PRIOR_WEIGHT * (jnp.log(d[0]) - jnp.log(p[0]))
    copy_grad = pltpu.make_async_copy(grad, grad_hbm, sems.at[3])
    copy_grad.start()
    copy_res.wait()
    copy_grad.wait()


def final_part(layers, density, prior, weight, e, o, tb, zb, obst, bodies, tfs, zfs, shis, slos, halos):
    rows, width = density.shape[1:]
    share = rows // layers
    padded = width + 2 * MARGIN
    args = [*in_hbm(density, prior, weight), e, o, tb, zb, obst, *bodies, *tfs, *zfs, *shis, *slos, *halos]
    return pl.pallas_call(
        lambda *refs: final_kernel(layers, *refs),
        out_shape=[jax.ShapeDtypeStruct((1, rows, width), F32), jax.ShapeDtypeStruct((COMPS, share, width), F32)],
        in_specs=[HBM] * 3 + [VMEM] * (len(args) - 3),
        out_specs=[HBM, HBM],
        scratch_shapes=[
            *[pltpu.VMEM((layers, COMPS, 2 * BLOCK, RANK * LANES), BF16)] * 2,
            *[pltpu.VMEM((COMPS, padded, LANES), BF16)] * 2,
            *[pltpu.VMEM((COMPS, width, RANK * LANES), BF16)] * 2,
            pltpu.VMEM((COMPS, rows, width), F32),
            pltpu.VMEM((COMPS, share, width), F32),
            *[pltpu.VMEM((1, rows, width), F32)] * 3,
            pltpu.VMEM((width, 2 * LANES), F32),
            pltpu.SMEM(weight.shape, F32),
            pltpu.SemaphoreType.DMA((5,)),
        ],
        compiler_params=limit(12 + 2 * layers),
        name="final",
    )(*args)


def body(density, prior, observed, filter_across, filter_along, comp_weight):
    layers, tiles = lax.axis_size("depth"), lax.axis_size("tile")
    both = ("depth", "tile")
    turns = [[(d, (d + s) % layers) for d in range(layers)] for s in range(layers)]
    inner = [(i, i ^ 1) for i in range(tiles)]
    outer = [(i, i + 1) for i in range(1, tiles - 1, 2)]
    outer += [(j, i) for i, j in outer]

    def outward(s):
        pairs = [(d * tiles + i, e * tiles + j) for d, e in turns[s] for i, j in outer]
        return pairs + [(d * tiles + t, (e if s else d ^ 1) * tiles + t) for d, e in turns[s] for t in (0, tiles - 1)]

    sent, observed = turn(density, filter_across, filter_along, observed)
    bodies = [sent] + [lax.ppermute(sent, "depth", pairs) for pairs in turns[1:]]
    out, out_other, inside = outer_part(sent, observed)
    from_o = lax.ppermute(out, both, outward(0))
    halos = [lax.ppermute(out_other, both, outward(s)) for s in range(1, layers)]
    tf, zf, tb, zb, shi, slo, obst = own_part(sent, observed)
    inside, _ = lax.optimization_barrier((inside, obst))
    from_e = lax.ppermute(inner_part(inside, bodies), "tile", inner)
    others = [other_part(received) for received in bodies[1:]]
    tfs, zfs, shis, slos = ([first] + [x[i] for x in others] for i, first in enumerate((tf, zf, shi, slo)))
    return tuple(
        final_part(layers, density, prior, comp_weight, from_e, from_o, tb, zb, obst, bodies, tfs, zfs, shis, slos, halos)
    )


def solution(mesh):
    placed = (
        P("depth", None, "tile"),
        P("depth", None, "tile"),
        P(None, None, "tile"),
        P("depth", None, None, None),
        P("depth", None, None, None),
        P(),
    )
    return jax.shard_map(
        body,
        mesh=mesh,
        in_specs=placed,
        out_specs=(P("depth", None, "tile"), P(None, "depth", "tile")),
        check_vma=False,
    )
```

```python
import jax
import jax.numpy as jnp
from jax import lax
from jax.experimental import pallas as pl
from jax.experimental.pallas import tpu as pltpu
from jax.sharding import PartitionSpec as P

COMPS = 6
RANK = 4
TAPS = 33
MARGIN = 16
HALO = 32
BLOCK = 32
LANES = 128
FILTERS = COMPS * RANK
ALONG_AT = 64
PRIOR_WEIGHT = 0.5
F32 = jnp.float32
BF16 = jnp.bfloat16
VMEM = pl.BlockSpec(memory_space=pltpu.VMEM)
HBM = pl.BlockSpec(memory_space=pltpu.HBM)


def split(x):
    hi = x.astype(BF16)
    return hi, (x - hi.astype(F32)).astype(BF16)


def in_hbm(*arrays):
    return [pltpu.with_memory_space_constraint(x, pltpu.HBM) for x in arrays]


def limit(mib):
    return pltpu.CompilerParams(vmem_limit_bytes=mib << 20)


def turn_kernel(d_hbm, fa_hbm, fl_hbm, o_hbm, body_ref, o_ref, d, fa, fl, sems):
    moves = ((fa_hbm, fa), (fl_hbm, fl), (d_hbm, d), (o_hbm, o_ref))
    copies = [pltpu.make_async_copy(a, b, sems.at[i]) for i, (a, b) in enumerate(moves)]
    for copy in copies:
        copy.start()
    for copy in copies[:3]:
        copy.wait()
    width = d.shape[2]
    body_ref[0:width, :] = d[0].T
    body_ref[width : width + FILTERS, :] = jnp.zeros((FILTERS, LANES), F32)
    for c in range(COMPS):
        rows = slice(width + RANK * c, width + RANK * (c + 1))
        body_ref[rows, 0:TAPS] = fa[0, c]
        body_ref[rows, ALONG_AT : ALONG_AT + TAPS] = fl[0, c]
    copies[3].wait()


def turn(density, across, along, observed):
    return pl.pallas_call(
        turn_kernel,
        out_shape=[
            jax.ShapeDtypeStruct((density.shape[2] + FILTERS, LANES), F32),
            jax.ShapeDtypeStruct(observed.shape, F32),
        ],
        in_specs=[HBM] * 4,
        out_specs=[VMEM] * 2,
        scratch_shapes=[pltpu.VMEM(x.shape, F32) for x in (density, across, along)] + [pltpu.SemaphoreType.DMA((4,))],
        compiler_params=limit(4),
        name="turn",
    )(*in_hbm(density, across, along, observed))


def is_even():
    return lax.rem(lax.axis_index("tile"), 2) == 0


def outer_edge(x):
    return jnp.where(is_even(), x[0:HALO, :], x[x.shape[0] - HALO : x.shape[0], :])


def inner_edge(x):
    return jnp.where(is_even(), x[x.shape[0] - HALO : x.shape[0], :], x[0:HALO, :])


def outer_kernel(body_ref, o_ref, out_ref, od_ref, in_ref):
    width = o_ref.shape[2]
    even = is_even()
    edge = outer_edge(body_ref.at[0:width])
    out_ref[0:HALO, :] = edge
    od_ref[...] = edge
    for c in range(COMPS):
        first = o_ref[c, :, 0:LANES].T[0:MARGIN]
        last = o_ref[c, :, width - LANES : width].T[LANES - MARGIN : LANES]
        out_ref[HALO + MARGIN * c : HALO + MARGIN * (c + 1), :] = jnp.where(even, first, last)
        in_ref[MARGIN * c : MARGIN * (c + 1), :] = jnp.where(even, last, first)


def outer_part(sent, observed):
    return pl.pallas_call(
        outer_kernel,
        out_shape=[
            jax.ShapeDtypeStruct((HALO + COMPS * MARGIN, LANES), F32),
            jax.ShapeDtypeStruct((HALO, LANES), F32),
            jax.ShapeDtypeStruct((COMPS * MARGIN, LANES), F32),
        ],
        in_specs=[VMEM] * 2,
        out_specs=[VMEM] * 3,
        compiler_params=limit(4),
        name="outer",
    )(sent, observed)


def inner_kernel(layers, *refs):
    obs_ref, bodies, out_ref = refs[0], refs[1:-1], refs[-1]
    width = bodies[0].shape[0] - FILTERS
    for l in range(layers):
        out_ref[HALO * l : HALO * (l + 1), :] = inner_edge(bodies[l].at[0:width])
    out_ref[HALO * layers :, :] = obs_ref[...]


def inner_part(edge, bodies):
    layers = len(bodies)
    return pl.pallas_call(
        lambda *refs: inner_kernel(layers, *refs),
        out_shape=jax.ShapeDtypeStruct((HALO * layers + COMPS * MARGIN, LANES), F32),
        in_specs=[VMEM] * (1 + layers),
        out_specs=VMEM,
        compiler_params=limit(4),
        name="inner",
    )(edge, *bodies)


def place(base, filters, first_tap, targets):
    tap = lax.broadcasted_iota(jnp.int32, (LANES, LANES), 0) - first_tap
    lane = lax.broadcasted_iota(jnp.int32, (LANES, LANES), 1)
    chosen = jnp.zeros((LANES, LANES), jnp.bool_)
    for target in targets(tap):
        chosen = chosen | (lane == target)
    chosen = (chosen & (tap >= 0) & (tap < TAPS)).astype(BF16)
    hi, lo = (jnp.dot(v, chosen, preferred_element_type=F32) for v in split(filters))
    base[...] = hi + lo


def along_blocks(base, dst, chosen=range(FILTERS)):
    for f in chosen:
        v = jnp.broadcast_to(base[f : f + 1, :], (BLOCK, LANES))
        v = pltpu.roll(v, 0, 1, stride=1, stride_axis=0)
        for p, part in enumerate(split(v)):
            dst[BLOCK * f : BLOCK * (f + 1), LANES * p : LANES * (p + 1)] = part


def across_blocks(base, dst, chosen=range(FILTERS)):
    row = lax.broadcasted_iota(jnp.int32, (MARGIN, LANES), 0)
    lane = lax.broadcasted_iota(jnp.int32, (MARGIN, LANES), 1)
    head, tail = lane <= row + MARGIN, lane >= row + LANES - 2 * MARGIN
    for f in chosen:
        v = jnp.broadcast_to(base[f : f + 1, :], (LANES, LANES))
        v = pltpu.roll(v, 0, 1, stride=1, stride_axis=0)
        v = jnp.concatenate(
            [jnp.where(head, v[:MARGIN], 0.0), v[MARGIN : LANES - MARGIN], jnp.where(tail, v[LANES - MARGIN :], 0.0)], axis=0
        )
        for p, part in enumerate(split(v)):
            dst[LANES * f : LANES * (f + 1), LANES * p : LANES * (p + 1)] = part


def forward_places(base, filters):
    place(base.at[0], filters, ALONG_AT, lambda k: (k, k + 64))
    place(base.at[1], filters, 0, lambda k: ((MARGIN - k) & (LANES - 1),))


def backward_places(base, filters):
    place(base.at[2], filters, ALONG_AT, lambda k: (TAPS - 1 - k, TAPS - 1 - k + 64))
    place(base.at[3], filters, 0, lambda k: ((k - MARGIN) & (LANES - 1),))


def stacked(windows):
    columns = [jnp.concatenate([hi, lo, hi, lo], axis=0) for hi, lo in windows]
    return jnp.concatenate(columns, axis=1) if len(columns) > 1 else columns[0]


def smooth(table, windows, stores):
    hi, lo = split(jnp.dot(table, stacked(windows), preferred_element_type=F32))
    for i, store in enumerate(stores):
        for f in range(table.shape[0] // BLOCK):
            part = (slice(BLOCK * f, BLOCK * (f + 1)), slice(LANES * i, LANES * (i + 1)))
            store(f, hi[part], lo[part])


def into(shi, slo, row):
    def store(f, hi, lo):
        c, r = divmod(f, RANK)
        at = (c, slice(row, row + BLOCK), slice(LANES * r, LANES * (r + 1)))
        shi[at] = hi
        slo[at] = lo

    return store


def forward_inside(body_ref, dhi, dlo, base, tf, zf, shi, slo):
    width = dhi.shape[0]
    dhi[...], dlo[...] = split(body_ref[0:width, :])
    along_blocks(base.at[0], tf)
    inside = width // BLOCK - 1
    window = lambda b: (dhi[BLOCK * b : BLOCK * b + 64, :], dlo[BLOCK * b : BLOCK * b + 64, :])
    starts = range(0, inside, 2)
    for n, b in enumerate(starts):
        group = range(b, min(b + 2, inside))
        smooth(tf[...], [window(i) for i in group], [into(shi, slo, BLOCK * i) for i in group])
        across_blocks(base.at[1], zf, range(n, FILTERS, len(starts)))


def own_kernel(body_ref, o_ref, tf, zf, tb, zb, shi, slo, obst, dhi, dlo, base):
    filters = body_ref[dhi.shape[0] :, :]
    forward_places(base, filters)
    backward_places(base, filters)
    forward_inside(body_ref, dhi, dlo, base, tf, zf, shi, slo)
    for c in range(COMPS):
        chosen = range(RANK * c, RANK * (c + 1))
        along_blocks(base.at[2], tb, chosen)
        across_blocks(base.at[3], zb, chosen)
        obst[c] = o_ref[c].T


def other_kernel(body_ref, tf, zf, shi, slo, dhi, dlo, base):
    forward_places(base, body_ref[dhi.shape[0] :, :])
    forward_inside(body_ref, dhi, dlo, base, tf, zf, shi, slo)


def tables(width):
    along = jax.ShapeDtypeStruct((FILTERS * BLOCK, 2 * LANES), BF16)
    across = jax.ShapeDtypeStruct((FILTERS * LANES, 2 * LANES), BF16)
    smoothed = jax.ShapeDtypeStruct((COMPS, width - BLOCK, RANK * LANES), BF16)
    scratch = [pltpu.VMEM((width, LANES), BF16)] * 2 + [pltpu.VMEM((4, FILTERS, LANES), F32)]
    return along, across, smoothed, scratch


def own_part(sent, observed):
    width = observed.shape[2]
    along, across, smoothed, scratch = tables(width)
    out = [along, across, along, across, smoothed, smoothed, jax.ShapeDtypeStruct((COMPS, width, LANES), F32)]
    return pl.pallas_call(
        own_kernel,
        out_shape=out,
        in_specs=[VMEM, VMEM],
        out_specs=[VMEM] * len(out),
        scratch_shapes=scratch,
        compiler_params=limit(8),
        cost_estimate=pl.CostEstimate(flops=2_000_000_000, bytes_accessed=4_000_000, transcendentals=0),
        name="own",
    )(sent, observed)


def other_part(received):
    width = received.shape[0] - FILTERS
    along, across, smoothed, scratch = tables(width)
    return pl.pallas_call(
        other_kernel,
        out_shape=[along, across, smoothed, smoothed],
        in_specs=[VMEM],
        out_specs=[VMEM] * 4,
        scratch_shapes=scratch,
        compiler_params=limit(8),
        cost_estimate=pl.CostEstimate(flops=2_000_000_000, bytes_accessed=4_000_000, transcendentals=0),
        name="other",
    )(received)


def final_kernel(layers, *refs):
    it = iter(refs)
    take = lambda k: [next(it) for _ in range(k)]
    d_hbm, p_hbm, w_hbm, e_ref, o_ref, tb, zb, obst = take(8)
    bodies, tfs, zfs, shis, slos = (take(layers) for _ in range(5))
    halos = take(layers - 1)
    grad_hbm, res_hbm = take(2)
    ehi, elo, rhi, rlo, bhi, blo, turned, res, d, p, grad, acc, w_ref, sems = take(14)
    copy_d = pltpu.make_async_copy(d_hbm, d, sems.at[0])
    copy_p = pltpu.make_async_copy(p_hbm, p, sems.at[1])
    copy_w = pltpu.make_async_copy(w_hbm, w_ref, sems.at[4])
    copy_w.start()
    copy_d.start()
    copy_p.start()
    tile, tiles = lax.axis_index("tile"), lax.axis_size("tile")
    even = is_even()
    has_left, has_right = tile > 0, tile < tiles - 1
    width = obst.shape[1]
    share = res.shape[1]
    padded = width + 2 * MARGIN
    for l in range(layers):
        from_e = e_ref[HALO * l : HALO * (l + 1), :]
        from_o = o_ref[0:HALO, :] if l == 0 else halos[l - 1][...]
        left = jnp.where(has_left, jnp.where(even, from_o, from_e), 0.0)
        right = jnp.where(has_right, jnp.where(even, from_e, from_o), 0.0)
        windows = [
            split(jnp.concatenate([left, bodies[l][0:HALO, :]], axis=0)),
            split(jnp.concatenate([bodies[l][width - HALO : width, :], right], axis=0)),
        ]
        smooth(tfs[l][...], windows, [into(ehi.at[l], elo.at[l], 0), into(ehi.at[l], elo.at[l], BLOCK)])

    first_row = lax.axis_index("depth") * share
    copy_w.wait()

    def forward(c):
        lhs, rhs = [], []
        for edge, inside in ((ehi, shis), (elo, slos)):
            for l in range(layers):
                lhs.append(jnp.concatenate([edge[l, c, 0:BLOCK, :], inside[l][c], edge[l, c, BLOCK : 2 * BLOCK, :]], axis=0))
                rhs.append(zfs[l][RANK * LANES * c : RANK * LANES * (c + 1), :])
        out = jnp.dot(jnp.concatenate(lhs, axis=1), jnp.concatenate(rhs, axis=0), preferred_element_type=F32)
        response = out[:, 0:LANES] + out[:, LANES : 2 * LANES]
        w = w_ref[c]
        center = (response[MARGIN : MARGIN + width] - obst[c]) * w
        from_o = o_ref[HALO + MARGIN * c : HALO + MARGIN * (c + 1), :]
        from_e = e_ref[HALO * layers + MARGIN * c : HALO * layers + MARGIN * (c + 1), :]
        left = jnp.where(even, from_o, from_e)
        right = jnp.where(even, from_e, from_o)
        left = jnp.where(has_left, (response[0:MARGIN] - left) * w, 0.0)
        right = jnp.where(has_right, (response[MARGIN + width : padded] - right) * w, 0.0)
        for at, part in ((0, left), (MARGIN, center), (MARGIN + width, right)):
            hi, lo = split(part)
            rhi[c, at : at + part.shape[0], :] = hi
            rlo[c, at : at + part.shape[0], :] = lo
        turned[c] = center.T
        res[c] = turned[c, pl.ds(first_row, share), :]

    def smooth_back(c):
        window = lambda b: (rhi[c, BLOCK * b : BLOCK * b + 64, :], rlo[c, BLOCK * b : BLOCK * b + 64, :])

        def store(b):
            def put(r, hi, lo):
                at = (c, slice(BLOCK * b, BLOCK * (b + 1)), slice(LANES * r, LANES * (r + 1)))
                bhi[at] = hi
                blo[at] = lo

            return put

        table = tb[RANK * BLOCK * c : RANK * BLOCK * (c + 1), :]
        for b in range(0, width // BLOCK, 2):
            smooth(table, [window(b), window(b + 1)], [store(b), store(b + 1)])

    def across(c):
        z = zb[RANK * LANES * c : RANK * LANES * (c + 1), :]
        return jnp.dot(jnp.concatenate([bhi[c], blo[c]], axis=1), jnp.concatenate([z, z], axis=0), preferred_element_type=F32)

    for c in range(COMPS + 2):
        if c < COMPS:
            forward(c)
        if c == COMPS - 1:
            copy_res = pltpu.make_async_copy(res, res_hbm, sems.at[2])
            copy_res.start()
        if c == 3:
            acc[...] = across(0)
        if 3 < c:
            acc[...] += across(c - 3)
        if 1 < c:
            smooth_back(c - 2)
    acc[...] += across(COMPS - 1)
    out = acc[...]
    adj = (out[:, 0:LANES] + out[:, LANES : 2 * LANES]).T
    copy_d.wait()
    copy_p.wait()
    grad[0] = adj + PRIOR_WEIGHT * (jnp.log(d[0]) - jnp.log(p[0]))
    copy_grad = pltpu.make_async_copy(grad, grad_hbm, sems.at[3])
    copy_grad.start()
    copy_res.wait()
    copy_grad.wait()


def final_part(layers, density, prior, weight, e, o, tb, zb, obst, bodies, tfs, zfs, shis, slos, halos):
    rows, width = density.shape[1:]
    share = rows // layers
    padded = width + 2 * MARGIN
    args = [*in_hbm(density, prior, weight), e, o, tb, zb, obst, *bodies, *tfs, *zfs, *shis, *slos, *halos]
    return pl.pallas_call(
        lambda *refs: final_kernel(layers, *refs),
        out_shape=[jax.ShapeDtypeStruct((1, rows, width), F32), jax.ShapeDtypeStruct((COMPS, share, width), F32)],
        in_specs=[HBM] * 3 + [VMEM] * (len(args) - 3),
        out_specs=[HBM, HBM],
        scratch_shapes=[
            *[pltpu.VMEM((layers, COMPS, 2 * BLOCK, RANK * LANES), BF16)] * 2,
            *[pltpu.VMEM((COMPS, padded, LANES), BF16)] * 2,
            *[pltpu.VMEM((COMPS, width, RANK * LANES), BF16)] * 2,
            pltpu.VMEM((COMPS, rows, width), F32),
            pltpu.VMEM((COMPS, share, width), F32),
            *[pltpu.VMEM((1, rows, width), F32)] * 3,
            pltpu.VMEM((width, 2 * LANES), F32),
            pltpu.SMEM(weight.shape, F32),
            pltpu.SemaphoreType.DMA((5,)),
        ],
        compiler_params=limit(12 + 2 * layers),
        name="final",
    )(*args)


def body(density, prior, observed, filter_across, filter_along, comp_weight):
    layers, tiles = lax.axis_size("depth"), lax.axis_size("tile")
    both = ("depth", "tile")
    turns = [[(d, (d + s) % layers) for d in range(layers)] for s in range(layers)]
    inner = [(i, i ^ 1) for i in range(tiles)]
    outer = [(i, i + 1) for i in range(1, tiles - 1, 2)]
    outer += [(j, i) for i, j in outer]

    def outward(s):
        pairs = [(d * tiles + i, e * tiles + j) for d, e in turns[s] for i, j in outer]
        return pairs + [(d * tiles + t, (e if s else d ^ 1) * tiles + t) for d, e in turns[s] for t in (0, tiles - 1)]

    sent, observed = turn(density, filter_across, filter_along, observed)
    bodies = [sent] + [lax.ppermute(sent, "depth", pairs) for pairs in turns[1:]]
    out, out_other, inside = outer_part(sent, observed)
    from_o = lax.ppermute(out, both, outward(0))
    halos = [lax.ppermute(out_other, both, outward(s)) for s in range(1, layers)]
    tf, zf, tb, zb, shi, slo, obst = own_part(sent, observed)
    inside, _ = lax.optimization_barrier((inside, obst))
    from_e = lax.ppermute(inner_part(inside, bodies), "tile", inner)
    others = [other_part(received) for received in bodies[1:]]
    tfs, zfs, shis, slos = ([first] + [x[i] for x in others] for i, first in enumerate((tf, zf, shi, slo)))
    return tuple(
        final_part(layers, density, prior, comp_weight, from_e, from_o, tb, zb, obst, bodies, tfs, zfs, shis, slos, halos)
    )


def solution(mesh):
    placed = (
        P("depth", None, "tile"),
        P("depth", None, "tile"),
        P(None, None, "tile"),
        P("depth", None, None, None),
        P("depth", None, None, None),
        P(),
    )
    return jax.shard_map(
        body,
        mesh=mesh,
        in_specs=placed,
        out_specs=(P("depth", None, "tile"), P(None, "depth", "tile")),
        check_vma=False,
    )
```

```python
import jax
import jax.numpy as jnp
from jax import lax
from jax.experimental import pallas as pl
from jax.experimental.pallas import tpu as pltpu
from jax.sharding import PartitionSpec as P

COMPS = 6
RANK = 4
TAPS = 33
MARGIN = 16
HALO = 32
BLOCK = 32
LANES = 128
FILTERS = COMPS * RANK
ALONG_AT = 64
PRIOR_WEIGHT = 0.5
F32 = jnp.float32
BF16 = jnp.bfloat16
VMEM = pl.BlockSpec(memory_space=pltpu.VMEM)
HBM = pl.BlockSpec(memory_space=pltpu.HBM)


def split(x):
    hi = x.astype(BF16)
    return hi, (x - hi.astype(F32)).astype(BF16)


def in_hbm(*arrays):
    return [pltpu.with_memory_space_constraint(x, pltpu.HBM) for x in arrays]


def limit(mib):
    return pltpu.CompilerParams(vmem_limit_bytes=mib << 20)


def turn_kernel(d_hbm, fa_hbm, fl_hbm, o_hbm, body_ref, o_ref, d, fa, fl, sems):
    moves = ((fa_hbm, fa), (fl_hbm, fl), (d_hbm, d), (o_hbm, o_ref))
    copies = [pltpu.make_async_copy(a, b, sems.at[i]) for i, (a, b) in enumerate(moves)]
    for copy in copies:
        copy.start()
    for copy in copies[:3]:
        copy.wait()
    width = d.shape[2]
    body_ref[0:width, :] = d[0].T
    body_ref[width : width + FILTERS, :] = jnp.zeros((FILTERS, LANES), F32)
    for c in range(COMPS):
        rows = slice(width + RANK * c, width + RANK * (c + 1))
        body_ref[rows, 0:TAPS] = fa[0, c]
        body_ref[rows, ALONG_AT : ALONG_AT + TAPS] = fl[0, c]
    copies[3].wait()


def turn(density, across, along, observed):
    return pl.pallas_call(
        turn_kernel,
        out_shape=[
            jax.ShapeDtypeStruct((density.shape[2] + FILTERS, LANES), F32),
            jax.ShapeDtypeStruct(observed.shape, F32),
        ],
        in_specs=[HBM] * 4,
        out_specs=[VMEM] * 2,
        scratch_shapes=[pltpu.VMEM(x.shape, F32) for x in (density, across, along)] + [pltpu.SemaphoreType.DMA((4,))],
        compiler_params=limit(4),
        name="turn",
    )(*in_hbm(density, across, along, observed))


def is_even():
    return lax.rem(lax.axis_index("tile"), 2) == 0


def outer_edge(x):
    return jnp.where(is_even(), x[0:HALO, :], x[x.shape[0] - HALO : x.shape[0], :])


def inner_edge(x):
    return jnp.where(is_even(), x[x.shape[0] - HALO : x.shape[0], :], x[0:HALO, :])


def outer_kernel(body_ref, o_ref, out_ref, in_ref):
    width = o_ref.shape[2]
    even = is_even()
    out_ref[0:HALO, :] = outer_edge(body_ref.at[0:width])
    for c in range(COMPS):
        first = o_ref[c, :, 0:LANES].T[0:MARGIN]
        last = o_ref[c, :, width - LANES : width].T[LANES - MARGIN : LANES]
        out_ref[HALO + MARGIN * c : HALO + MARGIN * (c + 1), :] = jnp.where(even, first, last)
        in_ref[MARGIN * c : MARGIN * (c + 1), :] = jnp.where(even, last, first)


def cut_kernel(body_ref, od_ref):
    od_ref[...] = outer_edge(body_ref.at[0 : body_ref.shape[0] - FILTERS])


def cut_part(sent):
    return pl.pallas_call(
        cut_kernel,
        out_shape=jax.ShapeDtypeStruct((HALO, LANES), F32),
        in_specs=[VMEM],
        out_specs=VMEM,
        compiler_params=limit(4),
        name="cut",
    )(sent)


def outer_part(sent, observed):
    return pl.pallas_call(
        outer_kernel,
        out_shape=[
            jax.ShapeDtypeStruct((HALO + COMPS * MARGIN, LANES), F32),
            jax.ShapeDtypeStruct((COMPS * MARGIN, LANES), F32),
        ],
        in_specs=[VMEM] * 2,
        out_specs=[VMEM] * 2,
        compiler_params=limit(4),
        name="outer",
    )(sent, observed)


def inner_kernel(layers, *refs):
    obs_ref, bodies, out_ref = refs[0], refs[1:-1], refs[-1]
    width = bodies[0].shape[0] - FILTERS
    for l in range(layers):
        out_ref[HALO * l : HALO * (l + 1), :] = inner_edge(bodies[l].at[0:width])
    out_ref[HALO * layers :, :] = obs_ref[...]


def inner_part(edge, bodies):
    layers = len(bodies)
    return pl.pallas_call(
        lambda *refs: inner_kernel(layers, *refs),
        out_shape=jax.ShapeDtypeStruct((HALO * layers + COMPS * MARGIN, LANES), F32),
        in_specs=[VMEM] * (1 + layers),
        out_specs=VMEM,
        compiler_params=limit(4),
        name="inner",
    )(edge, *bodies)


def place(base, filters, first_tap, targets):
    tap = lax.broadcasted_iota(jnp.int32, (LANES, LANES), 0) - first_tap
    lane = lax.broadcasted_iota(jnp.int32, (LANES, LANES), 1)
    chosen = jnp.zeros((LANES, LANES), jnp.bool_)
    for target in targets(tap):
        chosen = chosen | (lane == target)
    chosen = (chosen & (tap >= 0) & (tap < TAPS)).astype(BF16)
    hi, lo = (jnp.dot(v, chosen, preferred_element_type=F32) for v in split(filters))
    base[...] = hi + lo


def along_blocks(base, dst, chosen=range(FILTERS)):
    for f in chosen:
        v = jnp.broadcast_to(base[f : f + 1, :], (BLOCK, LANES))
        v = pltpu.roll(v, 0, 1, stride=1, stride_axis=0)
        for p, part in enumerate(split(v)):
            dst[BLOCK * f : BLOCK * (f + 1), LANES * p : LANES * (p + 1)] = part


def across_blocks(base, dst, chosen=range(FILTERS)):
    row = lax.broadcasted_iota(jnp.int32, (MARGIN, LANES), 0)
    lane = lax.broadcasted_iota(jnp.int32, (MARGIN, LANES), 1)
    head, tail = lane <= row + MARGIN, lane >= row + LANES - 2 * MARGIN
    for f in chosen:
        v = jnp.broadcast_to(base[f : f + 1, :], (LANES, LANES))
        v = pltpu.roll(v, 0, 1, stride=1, stride_axis=0)
        v = jnp.concatenate(
            [jnp.where(head, v[:MARGIN], 0.0), v[MARGIN : LANES - MARGIN], jnp.where(tail, v[LANES - MARGIN :], 0.0)], axis=0
        )
        for p, part in enumerate(split(v)):
            dst[LANES * f : LANES * (f + 1), LANES * p : LANES * (p + 1)] = part


def forward_places(base, filters):
    place(base.at[0], filters, ALONG_AT, lambda k: (k, k + 64))
    place(base.at[1], filters, 0, lambda k: ((MARGIN - k) & (LANES - 1),))


def backward_places(base, filters):
    place(base.at[2], filters, ALONG_AT, lambda k: (TAPS - 1 - k, TAPS - 1 - k + 64))
    place(base.at[3], filters, 0, lambda k: ((k - MARGIN) & (LANES - 1),))


def stacked(windows):
    columns = [jnp.concatenate([hi, lo, hi, lo], axis=0) for hi, lo in windows]
    return jnp.concatenate(columns, axis=1) if len(columns) > 1 else columns[0]


def smooth(table, windows, stores):
    hi, lo = split(jnp.dot(table, stacked(windows), preferred_element_type=F32))
    for i, store in enumerate(stores):
        for f in range(table.shape[0] // BLOCK):
            part = (slice(BLOCK * f, BLOCK * (f + 1)), slice(LANES * i, LANES * (i + 1)))
            store(f, hi[part], lo[part])


def into(shi, slo, row):
    def store(f, hi, lo):
        c, r = divmod(f, RANK)
        at = (c, slice(row, row + BLOCK), slice(LANES * r, LANES * (r + 1)))
        shi[at] = hi
        slo[at] = lo

    return store


def forward_inside(body_ref, dhi, dlo, base, tf, zf, shi, slo):
    width = dhi.shape[0]
    dhi[...], dlo[...] = split(body_ref[0:width, :])
    along_blocks(base.at[0], tf)
    inside = width // BLOCK - 1
    window = lambda b: (dhi[BLOCK * b : BLOCK * b + 64, :], dlo[BLOCK * b : BLOCK * b + 64, :])
    starts = range(0, inside, 2)
    for n, b in enumerate(starts):
        group = range(b, min(b + 2, inside))
        smooth(tf[...], [window(i) for i in group], [into(shi, slo, BLOCK * i) for i in group])
        across_blocks(base.at[1], zf, range(n, FILTERS, len(starts)))


def own_kernel(body_ref, o_ref, tf, zf, tb, zb, shi, slo, obst, dhi, dlo, base):
    filters = body_ref[dhi.shape[0] :, :]
    forward_places(base, filters)
    backward_places(base, filters)
    forward_inside(body_ref, dhi, dlo, base, tf, zf, shi, slo)
    for c in range(COMPS):
        chosen = range(RANK * c, RANK * (c + 1))
        along_blocks(base.at[2], tb, chosen)
        across_blocks(base.at[3], zb, chosen)
        obst[c] = o_ref[c].T


def other_kernel(body_ref, tf, zf, shi, slo, dhi, dlo, base):
    forward_places(base, body_ref[dhi.shape[0] :, :])
    forward_inside(body_ref, dhi, dlo, base, tf, zf, shi, slo)


def tables(width):
    along = jax.ShapeDtypeStruct((FILTERS * BLOCK, 2 * LANES), BF16)
    across = jax.ShapeDtypeStruct((FILTERS * LANES, 2 * LANES), BF16)
    smoothed = jax.ShapeDtypeStruct((COMPS, width - BLOCK, RANK * LANES), BF16)
    scratch = [pltpu.VMEM((width, LANES), BF16)] * 2 + [pltpu.VMEM((4, FILTERS, LANES), F32)]
    return along, across, smoothed, scratch


def own_part(sent, observed):
    width = observed.shape[2]
    along, across, smoothed, scratch = tables(width)
    out = [along, across, along, across, smoothed, smoothed, jax.ShapeDtypeStruct((COMPS, width, LANES), F32)]
    return pl.pallas_call(
        own_kernel,
        out_shape=out,
        in_specs=[VMEM, VMEM],
        out_specs=[VMEM] * len(out),
        scratch_shapes=scratch,
        compiler_params=limit(8),
        cost_estimate=pl.CostEstimate(flops=2_000_000_000, bytes_accessed=4_000_000, transcendentals=0),
        name="own",
    )(sent, observed)


def other_part(received):
    width = received.shape[0] - FILTERS
    along, across, smoothed, scratch = tables(width)
    return pl.pallas_call(
        other_kernel,
        out_shape=[along, across, smoothed, smoothed],
        in_specs=[VMEM],
        out_specs=[VMEM] * 4,
        scratch_shapes=scratch,
        compiler_params=limit(8),
        cost_estimate=pl.CostEstimate(flops=2_000_000_000, bytes_accessed=4_000_000, transcendentals=0),
        name="other",
    )(received)


def final_kernel(layers, *refs):
    it = iter(refs)
    take = lambda k: [next(it) for _ in range(k)]
    d_hbm, p_hbm, w_hbm, e_ref, o_ref, tb, zb, obst = take(8)
    bodies, tfs, zfs, shis, slos = (take(layers) for _ in range(5))
    halos = take(layers - 1)
    grad_hbm, res_hbm = take(2)
    ehi, elo, rhi, rlo, bhi, blo, turned, res, d, p, grad, acc, w_ref, sems = take(14)
    copy_d = pltpu.make_async_copy(d_hbm, d, sems.at[0])
    copy_p = pltpu.make_async_copy(p_hbm, p, sems.at[1])
    copy_w = pltpu.make_async_copy(w_hbm, w_ref, sems.at[4])
    copy_w.start()
    copy_d.start()
    copy_p.start()
    tile, tiles = lax.axis_index("tile"), lax.axis_size("tile")
    even = is_even()
    has_left, has_right = tile > 0, tile < tiles - 1
    width = obst.shape[1]
    share = res.shape[1]
    padded = width + 2 * MARGIN
    for l in range(layers):
        from_e = e_ref[HALO * l : HALO * (l + 1), :]
        from_o = o_ref[0:HALO, :] if l == 0 else halos[l - 1][...]
        left = jnp.where(has_left, jnp.where(even, from_o, from_e), 0.0)
        right = jnp.where(has_right, jnp.where(even, from_e, from_o), 0.0)
        windows = [
            split(jnp.concatenate([left, bodies[l][0:HALO, :]], axis=0)),
            split(jnp.concatenate([bodies[l][width - HALO : width, :], right], axis=0)),
        ]
        smooth(tfs[l][...], windows, [into(ehi.at[l], elo.at[l], 0), into(ehi.at[l], elo.at[l], BLOCK)])

    first_row = lax.axis_index("depth") * share
    copy_w.wait()

    def forward(c):
        lhs, rhs = [], []
        for edge, inside in ((ehi, shis), (elo, slos)):
            for l in range(layers):
                lhs.append(jnp.concatenate([edge[l, c, 0:BLOCK, :], inside[l][c], edge[l, c, BLOCK : 2 * BLOCK, :]], axis=0))
                rhs.append(zfs[l][RANK * LANES * c : RANK * LANES * (c + 1), :])
        out = jnp.dot(jnp.concatenate(lhs, axis=1), jnp.concatenate(rhs, axis=0), preferred_element_type=F32)
        response = out[:, 0:LANES] + out[:, LANES : 2 * LANES]
        w = w_ref[c]
        center = (response[MARGIN : MARGIN + width] - obst[c]) * w
        from_o = o_ref[HALO + MARGIN * c : HALO + MARGIN * (c + 1), :]
        from_e = e_ref[HALO * layers + MARGIN * c : HALO * layers + MARGIN * (c + 1), :]
        left = jnp.where(even, from_o, from_e)
        right = jnp.where(even, from_e, from_o)
        left = jnp.where(has_left, (response[0:MARGIN] - left) * w, 0.0)
        right = jnp.where(has_right, (response[MARGIN + width : padded] - right) * w, 0.0)
        for at, part in ((0, left), (MARGIN, center), (MARGIN + width, right)):
            hi, lo = split(part)
            rhi[c, at : at + part.shape[0], :] = hi
            rlo[c, at : at + part.shape[0], :] = lo
        turned[c] = center.T
        res[c] = turned[c, pl.ds(first_row, share), :]

    def smooth_back(c):
        window = lambda b: (rhi[c, BLOCK * b : BLOCK * b + 64, :], rlo[c, BLOCK * b : BLOCK * b + 64, :])

        def store(b):
            def put(r, hi, lo):
                at = (c, slice(BLOCK * b, BLOCK * (b + 1)), slice(LANES * r, LANES * (r + 1)))
                bhi[at] = hi
                blo[at] = lo

            return put

        table = tb[RANK * BLOCK * c : RANK * BLOCK * (c + 1), :]
        for b in range(0, width // BLOCK, 2):
            smooth(table, [window(b), window(b + 1)], [store(b), store(b + 1)])

    def across(c):
        z = zb[RANK * LANES * c : RANK * LANES * (c + 1), :]
        return jnp.dot(jnp.concatenate([bhi[c], blo[c]], axis=1), jnp.concatenate([z, z], axis=0), preferred_element_type=F32)

    for c in range(COMPS + 2):
        if c < COMPS:
            forward(c)
        if c == COMPS:
            copy_res = pltpu.make_async_copy(res, res_hbm, sems.at[2])
            copy_res.start()
        if c == 3:
            acc[...] = across(0)
        if 3 < c:
            acc[...] += across(c - 3)
        if 1 < c:
            smooth_back(c - 2)
    acc[...] += across(COMPS - 1)
    out = acc[...]
    adj = (out[:, 0:LANES] + out[:, LANES : 2 * LANES]).T
    copy_d.wait()
    copy_p.wait()
    grad[0] = adj + PRIOR_WEIGHT * (jnp.log(d[0]) - jnp.log(p[0]))
    copy_grad = pltpu.make_async_copy(grad, grad_hbm, sems.at[3])
    copy_grad.start()
    copy_res.wait()
    copy_grad.wait()


def final_part(layers, density, prior, weight, e, o, tb, zb, obst, bodies, tfs, zfs, shis, slos, halos):
    rows, width = density.shape[1:]
    share = rows // layers
    padded = width + 2 * MARGIN
    args = [*in_hbm(density, prior, weight), e, o, tb, zb, obst, *bodies, *tfs, *zfs, *shis, *slos, *halos]
    return pl.pallas_call(
        lambda *refs: final_kernel(layers, *refs),
        out_shape=[jax.ShapeDtypeStruct((1, rows, width), F32), jax.ShapeDtypeStruct((COMPS, share, width), F32)],
        in_specs=[HBM] * 3 + [VMEM] * (len(args) - 3),
        out_specs=[HBM, HBM],
        scratch_shapes=[
            *[pltpu.VMEM((layers, COMPS, 2 * BLOCK, RANK * LANES), BF16)] * 2,
            *[pltpu.VMEM((COMPS, padded, LANES), BF16)] * 2,
            *[pltpu.VMEM((COMPS, width, RANK * LANES), BF16)] * 2,
            pltpu.VMEM((COMPS, rows, width), F32),
            pltpu.VMEM((COMPS, share, width), F32),
            *[pltpu.VMEM((1, rows, width), F32)] * 3,
            pltpu.VMEM((width, 2 * LANES), F32),
            pltpu.SMEM(weight.shape, F32),
            pltpu.SemaphoreType.DMA((5,)),
        ],
        compiler_params=limit(12 + 2 * layers),
        name="final",
    )(*args)


def body(density, prior, observed, filter_across, filter_along, comp_weight):
    layers, tiles = lax.axis_size("depth"), lax.axis_size("tile")
    both = ("depth", "tile")
    turns = [[(d, (d + s) % layers) for d in range(layers)] for s in range(layers)]
    inner = [(i, i ^ 1) for i in range(tiles)]
    outer = [(i, i + 1) for i in range(1, tiles - 1, 2)]
    outer += [(j, i) for i, j in outer]

    def outward(s):
        pairs = [(d * tiles + i, e * tiles + j) for d, e in turns[s] for i, j in outer]
        return pairs + [(d * tiles + t, (e if s else d ^ 1) * tiles + t) for d, e in turns[s] for t in (0, tiles - 1)]

    sent, observed = turn(density, filter_across, filter_along, observed)
    bodies = [sent] + [lax.ppermute(sent, "depth", pairs) for pairs in turns[1:]]
    out_other = cut_part(sent)
    turned, _ = lax.optimization_barrier((sent, out_other))
    out, inside = outer_part(turned, observed)
    from_o = lax.ppermute(out, both, outward(0))
    halos = [lax.ppermute(out_other, both, outward(s)) for s in range(1, layers)]
    tf, zf, tb, zb, shi, slo, obst = own_part(sent, observed)
    inside, _ = lax.optimization_barrier((inside, obst))
    from_e = lax.ppermute(inner_part(inside, bodies), "tile", inner)
    others = [other_part(received) for received in bodies[1:]]
    tfs, zfs, shis, slos = ([first] + [x[i] for x in others] for i, first in enumerate((tf, zf, shi, slo)))
    return tuple(
        final_part(layers, density, prior, comp_weight, from_e, from_o, tb, zb, obst, bodies, tfs, zfs, shis, slos, halos)
    )


def solution(mesh):
    placed = (
        P("depth", None, "tile"),
        P("depth", None, "tile"),
        P(None, None, "tile"),
        P("depth", None, None, None),
        P("depth", None, None, None),
        P(),
    )
    return jax.shard_map(
        body,
        mesh=mesh,
        in_specs=placed,
        out_specs=(P("depth", None, "tile"), P(None, "depth", "tile")),
        check_vma=False,
    )
```

```python
import jax
import jax.numpy as jnp
from jax import lax
from jax.experimental import pallas as pl
from jax.experimental.pallas import tpu as pltpu
from jax.sharding import PartitionSpec as P

COMPS = 6
RANK = 4
TAPS = 33
MARGIN = 16
HALO = 32
BLOCK = 32
LANES = 128
FILTERS = COMPS * RANK
ALONG_AT = 64
PRIOR_WEIGHT = 0.5
F32 = jnp.float32
BF16 = jnp.bfloat16
VMEM = pl.BlockSpec(memory_space=pltpu.VMEM)
HBM = pl.BlockSpec(memory_space=pltpu.HBM)


def split(x):
    hi = x.astype(BF16)
    return hi, (x - hi.astype(F32)).astype(BF16)


def in_hbm(*arrays):
    return [pltpu.with_memory_space_constraint(x, pltpu.HBM) for x in arrays]


def limit(mib):
    return pltpu.CompilerParams(vmem_limit_bytes=mib << 20)


def turn_kernel(d_hbm, fa_hbm, fl_hbm, o_hbm, body_ref, o_ref, d, fa, fl, sems):
    moves = ((fa_hbm, fa), (fl_hbm, fl), (d_hbm, d), (o_hbm, o_ref))
    copies = [pltpu.make_async_copy(a, b, sems.at[i]) for i, (a, b) in enumerate(moves)]
    for copy in copies:
        copy.start()
    for copy in copies[:3]:
        copy.wait()
    width = d.shape[2]
    body_ref[0:width, :] = d[0].T
    body_ref[width : width + FILTERS, :] = jnp.zeros((FILTERS, LANES), F32)
    for c in range(COMPS):
        rows = slice(width + RANK * c, width + RANK * (c + 1))
        body_ref[rows, 0:TAPS] = fa[0, c]
        body_ref[rows, ALONG_AT : ALONG_AT + TAPS] = fl[0, c]
    copies[3].wait()


def turn(density, across, along, observed):
    return pl.pallas_call(
        turn_kernel,
        out_shape=[
            jax.ShapeDtypeStruct((density.shape[2] + FILTERS, LANES), F32),
            jax.ShapeDtypeStruct(observed.shape, F32),
        ],
        in_specs=[HBM] * 4,
        out_specs=[VMEM] * 2,
        scratch_shapes=[pltpu.VMEM(x.shape, F32) for x in (density, across, along)] + [pltpu.SemaphoreType.DMA((4,))],
        compiler_params=limit(4),
        name="turn",
    )(*in_hbm(density, across, along, observed))


def is_even():
    return lax.rem(lax.axis_index("tile"), 2) == 0


def outer_edge(x):
    return jnp.where(is_even(), x[0:HALO, :], x[x.shape[0] - HALO : x.shape[0], :])


def inner_edge(x):
    return jnp.where(is_even(), x[x.shape[0] - HALO : x.shape[0], :], x[0:HALO, :])


def outer_kernel(body_ref, o_ref, out_ref, in_ref):
    width = o_ref.shape[2]
    even = is_even()
    out_ref[0:HALO, :] = outer_edge(body_ref.at[0:width])
    for c in range(COMPS):
        first = o_ref[c, :, 0:LANES].T[0:MARGIN]
        last = o_ref[c, :, width - LANES : width].T[LANES - MARGIN : LANES]
        out_ref[HALO + MARGIN * c : HALO + MARGIN * (c + 1), :] = jnp.where(even, first, last)
        in_ref[MARGIN * c : MARGIN * (c + 1), :] = jnp.where(even, last, first)


def cut_kernel(body_ref, od_ref):
    od_ref[...] = outer_edge(body_ref.at[0 : body_ref.shape[0] - FILTERS])


def cut_part(sent):
    return pl.pallas_call(
        cut_kernel,
        out_shape=jax.ShapeDtypeStruct((HALO, LANES), F32),
        in_specs=[VMEM],
        out_specs=VMEM,
        compiler_params=limit(4),
        name="cut",
    )(sent)


def outer_part(sent, observed):
    return pl.pallas_call(
        outer_kernel,
        out_shape=[
            jax.ShapeDtypeStruct((HALO + COMPS * MARGIN, LANES), F32),
            jax.ShapeDtypeStruct((COMPS * MARGIN, LANES), F32),
        ],
        in_specs=[VMEM] * 2,
        out_specs=[VMEM] * 2,
        compiler_params=limit(4),
        name="outer",
    )(sent, observed)


def inner_kernel(layers, *refs):
    obs_ref, bodies, out_ref = refs[0], refs[1:-1], refs[-1]
    width = bodies[0].shape[0] - FILTERS
    for l in range(layers):
        out_ref[HALO * l : HALO * (l + 1), :] = inner_edge(bodies[l].at[0:width])
    out_ref[HALO * layers :, :] = obs_ref[...]


def inner_part(edge, bodies):
    layers = len(bodies)
    return pl.pallas_call(
        lambda *refs: inner_kernel(layers, *refs),
        out_shape=jax.ShapeDtypeStruct((HALO * layers + COMPS * MARGIN, LANES), F32),
        in_specs=[VMEM] * (1 + layers),
        out_specs=VMEM,
        compiler_params=limit(4),
        name="inner",
    )(edge, *bodies)


def place(base, filters, first_tap, targets):
    tap = lax.broadcasted_iota(jnp.int32, (LANES, LANES), 0) - first_tap
    lane = lax.broadcasted_iota(jnp.int32, (LANES, LANES), 1)
    chosen = jnp.zeros((LANES, LANES), jnp.bool_)
    for target in targets(tap):
        chosen = chosen | (lane == target)
    chosen = (chosen & (tap >= 0) & (tap < TAPS)).astype(BF16)
    hi, lo = (jnp.dot(v, chosen, preferred_element_type=F32) for v in split(filters))
    base[...] = hi + lo


def along_blocks(base, dst, chosen=range(FILTERS)):
    for f in chosen:
        v = jnp.broadcast_to(base[f : f + 1, :], (BLOCK, LANES))
        v = pltpu.roll(v, 0, 1, stride=1, stride_axis=0)
        for p, part in enumerate(split(v)):
            dst[BLOCK * f : BLOCK * (f + 1), LANES * p : LANES * (p + 1)] = part


def across_blocks(base, dst, chosen=range(FILTERS)):
    row = lax.broadcasted_iota(jnp.int32, (MARGIN, LANES), 0)
    lane = lax.broadcasted_iota(jnp.int32, (MARGIN, LANES), 1)
    head, tail = lane <= row + MARGIN, lane >= row + LANES - 2 * MARGIN
    for f in chosen:
        v = jnp.broadcast_to(base[f : f + 1, :], (LANES, LANES))
        v = pltpu.roll(v, 0, 1, stride=1, stride_axis=0)
        v = jnp.concatenate(
            [jnp.where(head, v[:MARGIN], 0.0), v[MARGIN : LANES - MARGIN], jnp.where(tail, v[LANES - MARGIN :], 0.0)], axis=0
        )
        for p, part in enumerate(split(v)):
            dst[LANES * f : LANES * (f + 1), LANES * p : LANES * (p + 1)] = part


def forward_places(base, filters):
    place(base.at[0], filters, ALONG_AT, lambda k: (k, k + 64))
    place(base.at[1], filters, 0, lambda k: ((MARGIN - k) & (LANES - 1),))


def backward_places(base, filters):
    place(base.at[2], filters, ALONG_AT, lambda k: (TAPS - 1 - k, TAPS - 1 - k + 64))
    place(base.at[3], filters, 0, lambda k: ((k - MARGIN) & (LANES - 1),))


def stacked(windows):
    columns = [jnp.concatenate([hi, lo, hi, lo], axis=0) for hi, lo in windows]
    return jnp.concatenate(columns, axis=1) if len(columns) > 1 else columns[0]


def smooth(table, windows, stores):
    hi, lo = split(jnp.dot(table, stacked(windows), preferred_element_type=F32))
    for i, store in enumerate(stores):
        for f in range(table.shape[0] // BLOCK):
            part = (slice(BLOCK * f, BLOCK * (f + 1)), slice(LANES * i, LANES * (i + 1)))
            store(f, hi[part], lo[part])


def into(shi, slo, row):
    def store(f, hi, lo):
        c, r = divmod(f, RANK)
        at = (c, slice(row, row + BLOCK), slice(LANES * r, LANES * (r + 1)))
        shi[at] = hi
        slo[at] = lo

    return store


def forward_inside(body_ref, dhi, dlo, base, tf, zf, shi, slo):
    width = dhi.shape[0]
    dhi[...], dlo[...] = split(body_ref[0:width, :])
    along_blocks(base.at[0], tf)
    inside = width // BLOCK - 1
    window = lambda b: (dhi[BLOCK * b : BLOCK * b + 64, :], dlo[BLOCK * b : BLOCK * b + 64, :])
    starts = range(0, inside, 2)
    for n, b in enumerate(starts):
        group = range(b, min(b + 2, inside))
        smooth(tf[...], [window(i) for i in group], [into(shi, slo, BLOCK * i) for i in group])
        across_blocks(base.at[1], zf, range(n, FILTERS, len(starts)))


def own_kernel(body_ref, o_ref, tf, zf, tb, zb, shi, slo, obst, dhi, dlo, base):
    filters = body_ref[dhi.shape[0] :, :]
    forward_places(base, filters)
    backward_places(base, filters)
    for c in range(COMPS):
        obst[c] = o_ref[c].T
    forward_inside(body_ref, dhi, dlo, base, tf, zf, shi, slo)
    for c in range(COMPS):
        chosen = range(RANK * c, RANK * (c + 1))
        along_blocks(base.at[2], tb, chosen)
        across_blocks(base.at[3], zb, chosen)


def other_kernel(body_ref, tf, zf, shi, slo, dhi, dlo, base):
    forward_places(base, body_ref[dhi.shape[0] :, :])
    forward_inside(body_ref, dhi, dlo, base, tf, zf, shi, slo)


def tables(width):
    along = jax.ShapeDtypeStruct((FILTERS * BLOCK, 2 * LANES), BF16)
    across = jax.ShapeDtypeStruct((FILTERS * LANES, 2 * LANES), BF16)
    smoothed = jax.ShapeDtypeStruct((COMPS, width - BLOCK, RANK * LANES), BF16)
    scratch = [pltpu.VMEM((width, LANES), BF16)] * 2 + [pltpu.VMEM((4, FILTERS, LANES), F32)]
    return along, across, smoothed, scratch


def own_part(sent, observed):
    width = observed.shape[2]
    along, across, smoothed, scratch = tables(width)
    out = [along, across, along, across, smoothed, smoothed, jax.ShapeDtypeStruct((COMPS, width, LANES), F32)]
    return pl.pallas_call(
        own_kernel,
        out_shape=out,
        in_specs=[VMEM, VMEM],
        out_specs=[VMEM] * len(out),
        scratch_shapes=scratch,
        compiler_params=limit(8),
        cost_estimate=pl.CostEstimate(flops=2_000_000_000, bytes_accessed=4_000_000, transcendentals=0),
        name="own",
    )(sent, observed)


def other_part(received):
    width = received.shape[0] - FILTERS
    along, across, smoothed, scratch = tables(width)
    return pl.pallas_call(
        other_kernel,
        out_shape=[along, across, smoothed, smoothed],
        in_specs=[VMEM],
        out_specs=[VMEM] * 4,
        scratch_shapes=scratch,
        compiler_params=limit(8),
        cost_estimate=pl.CostEstimate(flops=2_000_000_000, bytes_accessed=4_000_000, transcendentals=0),
        name="other",
    )(received)


def final_kernel(layers, *refs):
    it = iter(refs)
    take = lambda k: [next(it) for _ in range(k)]
    d_hbm, p_hbm, w_hbm, e_ref, o_ref, tb, zb, obst = take(8)
    bodies, tfs, zfs, shis, slos = (take(layers) for _ in range(5))
    halos = take(layers - 1)
    grad_hbm, res_hbm = take(2)
    ehi, elo, rhi, rlo, bhi, blo, turned, res, d, p, grad, acc, w_ref, sems = take(14)
    copy_d = pltpu.make_async_copy(d_hbm, d, sems.at[0])
    copy_p = pltpu.make_async_copy(p_hbm, p, sems.at[1])
    copy_w = pltpu.make_async_copy(w_hbm, w_ref, sems.at[4])
    copy_w.start()
    copy_d.start()
    copy_p.start()
    tile, tiles = lax.axis_index("tile"), lax.axis_size("tile")
    even = is_even()
    has_left, has_right = tile > 0, tile < tiles - 1
    width = obst.shape[1]
    share = res.shape[1]
    padded = width + 2 * MARGIN
    for l in range(layers):
        from_e = e_ref[HALO * l : HALO * (l + 1), :]
        from_o = o_ref[0:HALO, :] if l == 0 else halos[l - 1][...]
        left = jnp.where(has_left, jnp.where(even, from_o, from_e), 0.0)
        right = jnp.where(has_right, jnp.where(even, from_e, from_o), 0.0)
        windows = [
            split(jnp.concatenate([left, bodies[l][0:HALO, :]], axis=0)),
            split(jnp.concatenate([bodies[l][width - HALO : width, :], right], axis=0)),
        ]
        smooth(tfs[l][...], windows, [into(ehi.at[l], elo.at[l], 0), into(ehi.at[l], elo.at[l], BLOCK)])

    first_row = lax.axis_index("depth") * share
    copy_w.wait()

    def forward(c):
        lhs, rhs = [], []
        for edge, inside in ((ehi, shis), (elo, slos)):
            for l in range(layers):
                lhs.append(jnp.concatenate([edge[l, c, 0:BLOCK, :], inside[l][c], edge[l, c, BLOCK : 2 * BLOCK, :]], axis=0))
                rhs.append(zfs[l][RANK * LANES * c : RANK * LANES * (c + 1), :])
        out = jnp.dot(jnp.concatenate(lhs, axis=1), jnp.concatenate(rhs, axis=0), preferred_element_type=F32)
        response = out[:, 0:LANES] + out[:, LANES : 2 * LANES]
        w = w_ref[c]
        center = (response[MARGIN : MARGIN + width] - obst[c]) * w
        from_o = o_ref[HALO + MARGIN * c : HALO + MARGIN * (c + 1), :]
        from_e = e_ref[HALO * layers + MARGIN * c : HALO * layers + MARGIN * (c + 1), :]
        left = jnp.where(even, from_o, from_e)
        right = jnp.where(even, from_e, from_o)
        left = jnp.where(has_left, (response[0:MARGIN] - left) * w, 0.0)
        right = jnp.where(has_right, (response[MARGIN + width : padded] - right) * w, 0.0)
        for at, part in ((0, left), (MARGIN, center), (MARGIN + width, right)):
            hi, lo = split(part)
            rhi[c, at : at + part.shape[0], :] = hi
            rlo[c, at : at + part.shape[0], :] = lo
        turned[c] = center.T
        res[c] = turned[c, pl.ds(first_row, share), :]

    def smooth_back(c):
        window = lambda b: (rhi[c, BLOCK * b : BLOCK * b + 64, :], rlo[c, BLOCK * b : BLOCK * b + 64, :])

        def store(b):
            def put(r, hi, lo):
                at = (c, slice(BLOCK * b, BLOCK * (b + 1)), slice(LANES * r, LANES * (r + 1)))
                bhi[at] = hi
                blo[at] = lo

            return put

        table = tb[RANK * BLOCK * c : RANK * BLOCK * (c + 1), :]
        for b in range(0, width // BLOCK, 2):
            smooth(table, [window(b), window(b + 1)], [store(b), store(b + 1)])

    def across(c):
        z = zb[RANK * LANES * c : RANK * LANES * (c + 1), :]
        return jnp.dot(jnp.concatenate([bhi[c], blo[c]], axis=1), jnp.concatenate([z, z], axis=0), preferred_element_type=F32)

    for c in range(COMPS + 2):
        if c < COMPS:
            forward(c)
        if c == COMPS:
            copy_res = pltpu.make_async_copy(res, res_hbm, sems.at[2])
            copy_res.start()
        if c == 3:
            acc[...] = across(0)
        if 3 < c:
            acc[...] += across(c - 3)
        if 1 < c:
            smooth_back(c - 2)
    acc[...] += across(COMPS - 1)
    out = acc[...]
    adj = (out[:, 0:LANES] + out[:, LANES : 2 * LANES]).T
    copy_d.wait()
    copy_p.wait()
    grad[0] = adj + PRIOR_WEIGHT * (jnp.log(d[0]) - jnp.log(p[0]))
    copy_grad = pltpu.make_async_copy(grad, grad_hbm, sems.at[3])
    copy_grad.start()
    copy_res.wait()
    copy_grad.wait()


def final_part(layers, density, prior, weight, e, o, tb, zb, obst, bodies, tfs, zfs, shis, slos, halos):
    rows, width = density.shape[1:]
    share = rows // layers
    padded = width + 2 * MARGIN
    args = [*in_hbm(density, prior, weight), e, o, tb, zb, obst, *bodies, *tfs, *zfs, *shis, *slos, *halos]
    return pl.pallas_call(
        lambda *refs: final_kernel(layers, *refs),
        out_shape=[jax.ShapeDtypeStruct((1, rows, width), F32), jax.ShapeDtypeStruct((COMPS, share, width), F32)],
        in_specs=[HBM] * 3 + [VMEM] * (len(args) - 3),
        out_specs=[HBM, HBM],
        scratch_shapes=[
            *[pltpu.VMEM((layers, COMPS, 2 * BLOCK, RANK * LANES), BF16)] * 2,
            *[pltpu.VMEM((COMPS, padded, LANES), BF16)] * 2,
            *[pltpu.VMEM((COMPS, width, RANK * LANES), BF16)] * 2,
            pltpu.VMEM((COMPS, rows, width), F32),
            pltpu.VMEM((COMPS, share, width), F32),
            *[pltpu.VMEM((1, rows, width), F32)] * 3,
            pltpu.VMEM((width, 2 * LANES), F32),
            pltpu.SMEM(weight.shape, F32),
            pltpu.SemaphoreType.DMA((5,)),
        ],
        compiler_params=limit(12 + 2 * layers),
        name="final",
    )(*args)


def body(density, prior, observed, filter_across, filter_along, comp_weight):
    layers, tiles = lax.axis_size("depth"), lax.axis_size("tile")
    both = ("depth", "tile")
    turns = [[(d, (d + s) % layers) for d in range(layers)] for s in range(layers)]
    inner = [(i, i ^ 1) for i in range(tiles)]
    outer = [(i, i + 1) for i in range(1, tiles - 1, 2)]
    outer += [(j, i) for i, j in outer]

    def outward(s):
        pairs = [(d * tiles + i, e * tiles + j) for d, e in turns[s] for i, j in outer]
        return pairs + [(d * tiles + t, (e if s else d ^ 1) * tiles + t) for d, e in turns[s] for t in (0, tiles - 1)]

    sent, observed = turn(density, filter_across, filter_along, observed)
    bodies = [sent] + [lax.ppermute(sent, "depth", pairs) for pairs in turns[1:]]
    out_other = cut_part(sent)
    turned, _ = lax.optimization_barrier((sent, out_other))
    out, inside = outer_part(turned, observed)
    from_o = lax.ppermute(out, both, outward(0))
    halos = [lax.ppermute(out_other, both, outward(s)) for s in range(1, layers)]
    tf, zf, tb, zb, shi, slo, obst = own_part(sent, observed)
    inside, _ = lax.optimization_barrier((inside, obst))
    from_e = lax.ppermute(inner_part(inside, bodies), "tile", inner)
    others = [other_part(received) for received in bodies[1:]]
    tfs, zfs, shis, slos = ([first] + [x[i] for x in others] for i, first in enumerate((tf, zf, shi, slo)))
    return tuple(
        final_part(layers, density, prior, comp_weight, from_e, from_o, tb, zb, obst, bodies, tfs, zfs, shis, slos, halos)
    )


def solution(mesh):
    placed = (
        P("depth", None, "tile"),
        P("depth", None, "tile"),
        P(None, None, "tile"),
        P("depth", None, None, None),
        P("depth", None, None, None),
        P(),
    )
    return jax.shard_map(
        body,
        mesh=mesh,
        in_specs=placed,
        out_specs=(P("depth", None, "tile"), P(None, "depth", "tile")),
        check_vma=False,
    )
```
